32 devices in a mesh: bunch: 4 (over y, x), mp: 8 (over z, core).
Axes of the slice: x: 2, y: 2, z: 4, core: 2. Of those that a mesh axis runs over, the one named last changes fastest.
Arguments:
- phase_space: float32 [4, 64, 32768], P(None, 'bunch', 'mp')
- phase_advance: float32 [2, 64], P(None, 'bunch'), may hold values from 0.3 to 2.8
- centroid_history: float32 [2, 64, 64], P(None, None, 'bunch'), may hold values from -6 to 6
- lr_wake: float32 [4160], replicated, may hold values from -0.09375 to 0.09375
- sr_dipole: float32 [256, 256], replicated, may hold values from -24 to 24
- sr_quad: float32 [256, 256], replicated, may hold values from -24 to 24
- slice_ids: int32 [2, 64, 32768], P(None, 'bunch', 'mp'), may hold values from 0 to 255
Outputs:
- tracked: float32 [4, 64, 32768], P(None, 'bunch', 'mp')
- centroids: float32 [2, 2, 64], P(None, None, 'bunch')
The draws below stay inside these ranges and needn't reach their ends.
All inputs are finite; a program needn't handle non-finite values.
Results may differ from the reference program's by a relative error of at most 0.00019.
Values sent between devices are 32-bit elements; how exact they have to be, the bound alone decides.
No kernel may reach another device: no remote copies, remote signals or barrier semaphores. Data moves between devices by JAX's collectives and lax.ppermute only.
A program may use at most 64 MiB of HBM per device.

```python
import jax
import jax.numpy as jnp
from jax import lax

SLICES = 256
HISTORY = 64
TURNS = 2
BUNCHES = 64
MACRO = 32768
LAGS = 4160


def draw_phase_space(key, part):
    key_offset = jax.random.fold_in(key, 11)
    key_noise = jax.random.fold_in(key, 12)
    offsets = jax.random.normal(key_offset, (4, BUNCHES, 1), jnp.float32)
    ramp_up = 0.5 + jnp.arange(MACRO, dtype=jnp.float32) / MACRO
    noise_part = 0.5 * jax.random.normal(key_noise, (4, BUNCHES, MACRO), jnp.float32)
    return offsets * ramp_up[None, None, :] + noise_part


def touch_ends(result, stream_key, smallest, high):
    longest = result.shape.index(max(result.shape))
    spots = []
    for shift in (0, 1):
        where = [jax.random.randint(jax.random.fold_in(stream_key, axis), (), 0, length) for axis, length in enumerate(result.shape)]
        where[longest] = (where[longest] + shift) % result.shape[longest]
        spots.append(tuple(where))
    return result.at[spots[0]].set(smallest).at[spots[1]].set(high)


def level_of(stream_key, extent, shards, least, top_value):
    factor_of, own = 1.0, jax.random.fold_in(stream_key, 6)
    for dim, parts in shards:
        steps = jnp.exp(jax.random.uniform(jax.random.fold_in(own, dim), (parts,), jnp.float32, least / len(shards), top_value / len(shards)))
        factor_of = factor_of * jnp.repeat(steps, extent[dim] // parts).reshape([-1 if axis == dim else 1 for axis in range(len(extent))])
    return factor_of


def scatter_about(stream_key, extent, deviation, most, cuts=(), kind=jnp.bfloat16):
    loudness = level_of(stream_key, extent, cuts, -0.22, 0.18) if cuts else 1.0
    entries = jax.random.normal(stream_key, extent, jnp.float32) * deviation * loudness
    return jnp.minimum(jnp.maximum(entries, -most), most).astype(kind)


def setup_inputs(seed: int = 0) -> dict:
    splits = jax.random.split(jax.random.key(seed), 8)
    phase_space = draw_phase_space(jax.random.fold_in(splits[7], 71), 0)
    phase_advance = jnp.clip(0.3 + 2.5 * jax.random.uniform(splits[1], (2, BUNCHES), jnp.float32) ** level_of(splits[1], (2, BUNCHES), ((1, 4),), -0.2, 0.2), 0.3, 2.8)
    centroid_history = scatter_about(splits[2], (2, HISTORY, BUNCHES), 1.0, 6.0, ((2, 4),), jnp.float32)
    lr_wake = scatter_about(splits[3], (LAGS,), LAGS ** -0.5, 0.09375, (), jnp.float32)
    sr_dipole = scatter_about(splits[4], (SLICES, SLICES), 4.0, 24.0, (), jnp.float32)
    sr_quad = scatter_about(splits[5], (SLICES, SLICES), 4.0, 24.0, (), jnp.float32)
    slice_ids = touch_ends(jax.random.randint(splits[6], (TURNS, BUNCHES, MACRO), 0, SLICES), jax.random.fold_in(splits[6], 1), 0, SLICES - 1).astype(jnp.int32)
    return {"phase_space": phase_space, "phase_advance": phase_advance, "centroid_history": centroid_history, "lr_wake": lr_wake, "sr_dipole": sr_dipole, "sr_quad": sr_quad, "slice_ids": slice_ids}


DETUNE = 0.02


def reference(phase_space, phase_advance, centroid_history, lr_wake, sr_dipole, sr_quad, slice_ids):
    highest = lax.Precision.HIGHEST
    all_bunches = phase_space.shape[1]
    macro_total = phase_space.shape[2]
    length = (HISTORY + 1) * all_bunches
    padded = jnp.concatenate([jnp.zeros((all_bunches,), jnp.float32), lr_wake])
    starts = jnp.arange(all_bunches, dtype=jnp.int32)
    windows = jax.vmap(lambda start_at: lax.dynamic_slice(padded, (start_at,), (length,)))(starts)
    history = centroid_history
    coords = phase_space
    centroid_rows = []
    offsets = (jnp.arange(all_bunches, dtype=jnp.int32) * SLICES)[:, None]
    segments_total = all_bunches * SLICES
    for turn_index in range(TURNS):
        slice_row = slice_ids[turn_index]
        segment = (slice_row + offsets).reshape(-1)
        counts = jax.ops.segment_sum(jnp.ones((segment.shape[0],), jnp.float32), segment, segments_total)
        sum_x = jax.ops.segment_sum(coords[0].reshape(-1), segment, segments_total)
        sum_y = jax.ops.segment_sum(coords[2].reshape(-1), segment, segments_total)
        density = counts.reshape(all_bunches, SLICES) / macro_total
        dipole = jnp.stack([sum_x, sum_y]).reshape(2, all_bunches, SLICES) / macro_total
        centroid = jnp.sum(dipole, axis=2)
        centroid_rows.append(centroid)
        dip_kick = jnp.einsum("pbj,ij->pbi", dipole, sr_dipole, precision=highest)
        quad_kick = jnp.einsum("bj,ij->bi", density, sr_quad, precision=highest)
        all_rows = jnp.concatenate([centroid[:, None, :], history], axis=1)[:, :, ::-1].reshape(2, length)
        far_kick = jnp.einsum("bk,pk->pb", windows, all_rows, precision=highest)
        slice_dip = jnp.take_along_axis(dip_kick, jnp.broadcast_to(slice_row[None], (2,) + slice_row.shape), axis=2)
        slice_quad = jnp.take_along_axis(quad_kick, slice_row, axis=1)
        coord_x, moment_x, coord_y, moment_y = coords[0], coords[1], coords[2], coords[3]
        moment_x = moment_x + slice_dip[0] + slice_quad * coord_x + far_kick[0][:, None]
        moment_y = moment_y + slice_dip[1] - slice_quad * coord_y + far_kick[1][:, None]
        action = coord_x * coord_x + moment_x * moment_x + coord_y * coord_y + moment_y * moment_y
        angle_x = phase_advance[0][:, None] + DETUNE * action
        angle_y = phase_advance[1][:, None] + DETUNE * action
        new_x = jnp.cos(angle_x) * coord_x + jnp.sin(angle_x) * moment_x
        new_mx = -jnp.sin(angle_x) * coord_x + jnp.cos(angle_x) * moment_x
        new_y = jnp.cos(angle_y) * coord_y + jnp.sin(angle_y) * moment_y
        new_my = -jnp.sin(angle_y) * coord_y + jnp.cos(angle_y) * moment_y
        coords = jnp.stack([new_x, new_mx, new_y, new_my])
        history = jnp.concatenate([centroid[:, None, :], history[:, :-1]], axis=1)
    return coords, jnp.stack(centroid_rows, axis=1)
```

```python
import functools

import jax
import jax.numpy as jnp
from jax import lax
from jax.experimental import pallas as pl
from jax.experimental.pallas import tpu as pltpu
from jax.sharding import PartitionSpec as P

SLICES = 256
TURNS = 2
DETUNE = 0.02
LOW = 32
HIGH = SLICES // LOW
HIGHEST = lax.Precision.HIGHEST
F32 = jnp.float32


def iota(shape, axis):
    return lax.broadcasted_iota(jnp.int32, shape, axis)


def rows_to_column(row, offset, count):
    length = row.shape[1]
    pick = iota((count, length), 1) == iota((count, length), 0) + offset
    return jnp.sum(jnp.where(pick, jnp.broadcast_to(row, (count, length)), 0.0), axis=1, keepdims=True)


def column_to_row(column):
    count = column.shape[0]
    eye = iota((count, count), 1) == iota((count, count), 0)
    return jnp.sum(jnp.where(eye, jnp.broadcast_to(column, (count, count)), 0.0), axis=0, keepdims=True)


def spread_far(weighted, offset):
    own, width = weighted.shape
    rows = iota((own, width), 0)
    step = 1
    while step < own:
        weighted = jnp.where((rows & step) != 0, pltpu.roll(weighted, step, 1), weighted)
        step *= 2
    return pltpu.roll(jnp.sum(weighted, axis=0, keepdims=True), width // 2 + 1 + offset, 1)


def wake_rows(wake_ref):
    depth1, all_bunches = wake_ref.shape
    wake = wake_ref[...]
    zero = jnp.zeros((1, all_bunches), F32)
    before = jnp.concatenate([zero, wake[:-1]], axis=0)
    return jnp.concatenate([before, wake], axis=1)


def start_kernel(x_ref, y_ref, history_ref, wake_ref, small_ref):
    own = x_ref.shape[0]
    offset = lax.axis_index("bunch") * own
    macro_total = x_ref.shape[1] * lax.axis_size("mp")
    lags = wake_rows(wake_ref)
    depth = history_ref.shape[1]
    mine = jnp.where(lax.axis_index("mp") == 0, 1.0, 0.0).astype(F32)
    centroids = [
        jnp.sum(x_ref[...], axis=1, keepdims=True) / macro_total,
        jnp.sum(y_ref[...], axis=1, keepdims=True) / macro_total,
    ]
    rows = []
    for turn in range(TURNS):
        for plane in range(2):
            kept = depth - turn
            older = lax.dot_general(
                history_ref[plane, :kept],
                lags[1 + turn : 1 + turn + kept],
                (((0,), (0,)), ((), ())),
                precision=HIGHEST,
                preferred_element_type=F32,
            )
            weighted = centroids[plane] * lags[turn : turn + 1] + mine * older
            rows.append(spread_far(weighted, offset))
    rows.append(jnp.zeros((small_ref.shape[0] - len(rows), rows[0].shape[1]), F32))
    small_ref[...] = jnp.concatenate(rows, axis=0)


def moments_kernel(x_ref, y_ref, slice_ref, out_ref, split_ref, block_ref):
    own, macros = x_ref.shape
    for index, ref in enumerate((x_ref, y_ref)):
        whole = ref[...]
        upper = whole.astype(jnp.bfloat16).astype(F32)
        split_ref[2 * index] = upper
        split_ref[2 * index + 1] = whole - upper
    chunk = min(1024, macros)
    low_levels = iota((LOW, chunk), 0)
    high_levels = iota((HIGH, chunk), 0)

    def one_bunch(bunch, carry):
        total = jnp.zeros((5 * HIGH, LOW), F32)
        for start in range(0, macros, chunk):
            span = pl.ds(start, chunk)
            ids = slice_ref[pl.ds(bunch, 1), span]
            low = jnp.broadcast_to(ids & (LOW - 1), (LOW, chunk)) == low_levels
            high = jnp.broadcast_to(ids // LOW, (HIGH, chunk)) == high_levels
            parts = [jnp.where(high, 1.0, 0.0)]
            for part in range(4):
                line = jnp.broadcast_to(split_ref[part, pl.ds(bunch, 1), span], (HIGH, chunk))
                parts.append(jnp.where(high, line, 0.0))
            total += lax.dot_general(
                jnp.concatenate(parts, axis=0).astype(jnp.bfloat16),
                low.astype(F32).astype(jnp.bfloat16),
                (((1,), (1,)), ((), ())),
                preferred_element_type=F32,
            )
        block_ref[bunch, 0] = total[:HIGH]
        block_ref[bunch, 1] = total[HIGH : 2 * HIGH] + total[2 * HIGH : 3 * HIGH]
        block_ref[bunch, 2] = total[3 * HIGH : 4 * HIGH] + total[4 * HIGH :]
        return carry

    lax.fori_loop(0, own, one_bunch, 0)
    for kind in range(3):
        out_ref[kind] = jnp.concatenate([block_ref[:, kind, level, :] for level in range(HIGH)], axis=1)


def sincos(angle):
    turns = jnp.floor(angle * 0.6366197723675814 + 0.5)
    rest = angle - turns * 1.5703125
    rest = rest - turns * 4.8351287841796875e-4
    rest = rest - turns * 3.13855707645416259765625e-7
    rest = rest - turns * 6.077100628276710381e-11
    rest = jnp.clip(rest, -1.0, 1.0)
    square = rest * rest
    sine = rest + rest * square * (-1.6666654611e-1 + square * (8.3321608736e-3 - square * 1.9515295891e-4))
    cosine = (
        1.0
        - 0.5 * square
        + square * square * (4.166664568298827e-2 + square * (-1.388731625493765e-3 + square * 2.443315711809948e-5))
    )
    quadrant = turns.astype(jnp.int32)
    swap = (quadrant & 1) != 0
    out_sine = jnp.where(swap, cosine, sine)
    out_cosine = jnp.where(swap, sine, cosine)
    out_sine = jnp.where((quadrant & 2) != 0, -out_sine, out_sine)
    out_cosine = jnp.where(((quadrant + 1) & 2) != 0, -out_cosine, out_cosine)
    return out_sine, out_cosine


def apply_kernel(turn, senders, *refs):
    last = turn == TURNS - 1
    coords_ref, slice_ref, advance_ref, dipole_wake_ref, quad_wake_ref, wake_ref = refs[:6]
    moment_refs = refs[6 : 6 + senders]
    small_refs = refs[6 + senders : 6 + 2 * senders]
    rest_refs = refs[6 + 2 * senders :]
    _, own, macros = coords_ref.shape
    offset = lax.axis_index("bunch") * own
    macro_total = macros * lax.axis_size("mp")
    moments = functools.reduce(lambda a, b: a + b, [ref[...] for ref in moment_refs]) / macro_total
    small = functools.reduce(lambda a, b: a + b, [ref[...] for ref in small_refs])
    if last:
        earlier_row_ref, earlier_centroid_ref, out_ref, centroid_ref = rest_refs[:4]
    else:
        out_ref, centroid_ref, small_out_ref = rest_refs[:3]
    flat_dipole = moments[1:].reshape(2 * own, SLICES)
    contract = (((1,), (1,)), ((), ()))
    dip_kick = lax.dot_general(
        flat_dipole, dipole_wake_ref[...], contract, precision=HIGHEST, preferred_element_type=F32
    )
    quad_kick = lax.dot_general(
        moments[0], quad_wake_ref[...], contract, precision=HIGHEST, preferred_element_type=F32
    )
    far = []
    for plane in range(2):
        row = small[plane : plane + 1]
        if last:
            row = row + earlier_row_ref[2 + plane : 3 + plane]
        far.append(rows_to_column(row, offset, own))
    kick_x = dip_kick[:own] + far[0]
    kick_y = dip_kick[own:] + far[1]
    tables = (kick_x, kick_y, quad_kick)
    centroid = jnp.concatenate(
        [column_to_row(jnp.sum(moments[1 + plane], axis=1, keepdims=True)) for plane in range(2)], axis=0
    )
    if last:
        for plane in range(2):
            centroid_ref[plane] = jnp.concatenate(
                [earlier_centroid_ref[plane : plane + 1], centroid[plane : plane + 1]], axis=0
            )
    else:
        centroid_ref[...] = centroid
    turned = []
    for plane in range(2):
        line = advance_ref[plane : plane + 1, :]
        turned.append((rows_to_column(jnp.sin(line), 0, own), rows_to_column(jnp.cos(line), 0, own)))

    chunk = min(512, macros)

    def pick(table, within, upper):
        halves = [
            jnp.take_along_axis(
                jnp.broadcast_to(table[:, None, half * 128 : half * 128 + 128], (own, 1, 128)).reshape(own, 128),
                within,
                axis=1,
            )
            for half in range(2)
        ]
        return jnp.where(upper, halves[1], halves[0])

    def step(index, sums):
        for start in range(0, chunk, 128):
            span = pl.ds(pl.multiple_of(index * chunk + start, 128), 128)
            ids = slice_ref[:, span]
            within = ids & 127
            upper = ids >= 128
            picked = [pick(table, within, upper) for table in tables]
            x, mx, y, my = (coords_ref[row, :, span] for row in range(4))
            mx = mx + picked[0] + picked[2] * x
            my = my + picked[1] - picked[2] * y
            action = x * x + mx * mx + y * y + my * my
            sine, cosine = sincos(DETUNE * action)
            new_sums = []
            for plane, (u, v) in enumerate(((x, mx), (y, my))):
                sine_0, cosine_0 = turned[plane]
                full_sine = sine_0 * cosine + cosine_0 * sine
                full_cosine = cosine_0 * cosine - sine_0 * sine
                new_u = full_cosine * u + full_sine * v
                out_ref[2 * plane, :, span] = new_u
                out_ref[2 * plane + 1, :, span] = full_cosine * v - full_sine * u
                new_sums.append(sums[plane] + new_u)
            sums = tuple(new_sums)
        return sums

    zero = jnp.zeros((own, 128), F32)
    sums = lax.fori_loop(0, macros // chunk, step, (zero, zero))
    if not last:
        lags = wake_rows(wake_ref)
        rows = [
            spread_far(jnp.sum(sums[plane], axis=1, keepdims=True) / macro_total * lags[:1], offset)
            for plane in range(2)
        ]
        rows.append(jnp.zeros((small_out_ref.shape[0] - 2, rows[0].shape[1]), F32))
        small_out_ref[...] = jnp.concatenate(rows, axis=0)


def whole_spec(shape):
    return pl.BlockSpec(shape, lambda i: (0,) * len(shape))


def row_spec(shape, row):
    return pl.BlockSpec((pl.Squeezed(),) + shape[1:], lambda i: (row,) + (0,) * (len(shape) - 1))


def exchange(value, axis, steps):
    size = lax.axis_size(axis)
    return [lax.ppermute(value, axis, [(source, source ^ step) for source in range(size)]) for step in steps]


def body(phase_space, phase_advance, centroid_history, lr_wake, sr_dipole, sr_quad, slice_ids):
    _, own, macros = phase_space.shape
    depth = centroid_history.shape[1]
    bunch_shards = lax.axis_size("bunch")
    macro_shards = lax.axis_size("mp")
    all_bunches = own * bunch_shards
    wake = lr_wake.reshape(depth + 1, all_bunches)
    small_shape = jax.ShapeDtypeStruct((8, 2 * all_bunches), F32)
    moment_shape = jax.ShapeDtypeStruct((3, own, SLICES), F32)

    small = pl.pallas_call(
        start_kernel,
        out_shape=small_shape,
        in_specs=[
            row_spec(phase_space.shape, 0),
            row_spec(phase_space.shape, 2),
            whole_spec(centroid_history.shape),
            whole_spec(wake.shape),
        ],
        out_specs=whole_spec(small_shape.shape),
        grid=(1,),
        name="start",
    )(phase_space, phase_space, centroid_history, wake)

    coords = phase_space
    earlier_small = earlier_centroid = None
    for turn in range(TURNS):
        moments = pl.pallas_call(
            moments_kernel,
            out_shape=moment_shape,
            in_specs=[
                row_spec(coords.shape, 0),
                row_spec(coords.shape, 2),
                row_spec(slice_ids.shape, turn),
            ],
            scratch_shapes=[
                pltpu.VMEM((4, own, macros), F32),
                pltpu.VMEM((own, 3, HIGH, LOW), F32),
            ],
            out_specs=whole_spec(moment_shape.shape),
            grid=(1,),
            name="moments",
        )(coords, coords, slice_ids)
        for received in exchange(small, "bunch", range(bunch_shards - 1, 0, -1)):
            small = small + received
        moments = moments + exchange(moments, "mp", [1])[0]
        small = small + exchange(small, "mp", [1])[0]
        steps = range(macro_shards - 2, 0, -2)
        all_moments = [moments] + exchange(moments, "mp", steps)
        all_small = [small] + exchange(small, "mp", steps)
        senders = len(all_moments)
        last = turn == TURNS - 1
        operands = [coords, slice_ids, phase_advance, sr_dipole, sr_quad, wake]
        specs = [whole_spec(coords.shape), row_spec(slice_ids.shape, turn)]
        specs += [whole_spec(operand.shape) for operand in operands[2:]]
        operands += all_moments + all_small
        specs += [whole_spec(moments.shape)] * senders + [whole_spec(small.shape)] * senders
        coords_shape = jax.ShapeDtypeStruct(coords.shape, F32)
        if last:
            operands += [earlier_small, earlier_centroid]
            specs += [whole_spec(earlier_small.shape), whole_spec(earlier_centroid.shape)]
            outs = (coords_shape, jax.ShapeDtypeStruct((2, TURNS, own), F32))
        else:
            outs = (coords_shape, jax.ShapeDtypeStruct((2, own), F32), small_shape)
        results = pl.pallas_call(
            functools.partial(apply_kernel, turn, senders),
            out_shape=outs,
            in_specs=specs,
            out_specs=tuple(whole_spec(out.shape) for out in outs),
            grid=(1,),
            name="apply" + str(turn),
        )(*operands)
        if last:
            coords, centroids = results
        else:
            earlier_small = functools.reduce(lambda a, b: a + b, all_small)
            coords, earlier_centroid, small = results
    return coords, centroids


def solution(mesh):
    placed = (
        P(None, "bunch", "mp"),
        P(None, "bunch"),
        P(None, None, "bunch"),
        P(),
        P(),
        P(),
        P(None, "bunch", "mp"),
    )
    return jax.shard_map(
        body,
        mesh=mesh,
        in_specs=placed,
        out_specs=(P(None, "bunch", "mp"), P(None, None, "bunch")),
        check_vma=False,
    )
```

```python
import functools

import jax
import jax.numpy as jnp
from jax import lax
from jax.experimental import pallas as pl
from jax.experimental.pallas import tpu as pltpu
from jax.sharding import PartitionSpec as P

SLICES = 256
TURNS = 2
DETUNE = 0.02
LOW = 32
HIGH = SLICES // LOW
LANES = 128
SUBLANES = 8
HALVES = SLICES // LANES
CORES = 2
HIGHEST = lax.Precision.HIGHEST
F32 = jnp.float32
BF16 = jnp.bfloat16


def iota(shape, axis):
    return lax.broadcasted_iota(jnp.int32, shape, axis)


def total(values):
    return functools.reduce(lambda a, b: a + b, values)


def rows_to_column(row, offset, count):
    length = row.shape[1]
    pick = iota((count, length), 1) == iota((count, length), 0) + offset
    return jnp.sum(jnp.where(pick, jnp.broadcast_to(row, (count, length)), 0.0), axis=1, keepdims=True)


def column_to_row(column, offset, length):
    count = column.shape[0]
    pick = iota((count, length), 1) == iota((count, length), 0) + offset
    return jnp.sum(jnp.where(pick, jnp.broadcast_to(column, (count, length)), 0.0), axis=0, keepdims=True)


def spread_far(weighted, offset):
    own, width = weighted.shape
    rows = iota((own, width), 0)
    step = 1
    while step < own:
        weighted = jnp.where((rows & step) != 0, pltpu.roll(weighted, step, 1), weighted)
        step *= 2
    return pltpu.roll(jnp.sum(weighted, axis=0, keepdims=True), width // 2 + 1 + offset, 1)


def gather_lanes(row, index):
    count = index.shape[0]
    result = jnp.zeros(index.shape, F32)
    for tile in range(row.shape[1] // LANES):
        part = jnp.broadcast_to(row[:, tile * LANES : (tile + 1) * LANES], (count, LANES))
        taken = jnp.take_along_axis(part, index & (LANES - 1), axis=1)
        result = jnp.where(index // LANES == tile, taken, result)
    return result


def store_centroids(small_ref, columns, offset):
    tiles = small_ref.shape[0] // SUBLANES
    rows = [column_to_row(column, offset, tiles * LANES) for column in columns]
    rows.append(jnp.zeros((SUBLANES - len(rows), tiles * LANES), F32))
    whole = jnp.concatenate(rows, axis=0)
    for tile in range(tiles):
        small_ref[tile * SUBLANES : (tile + 1) * SUBLANES, :] = whole[:, tile * LANES : (tile + 1) * LANES]


def wake_rows(wake):
    before = jnp.concatenate([jnp.zeros((1, wake.shape[1]), F32), wake[:-1]], axis=0)
    return jnp.concatenate([before, wake], axis=1)


def store_split(split_ref, plane, block, bunches, values):
    upper = values.astype(BF16).astype(F32)
    split_ref[2 * plane, block, bunches, :] = upper
    split_ref[2 * plane + 1, block, bunches, :] = values - upper


def store_digits(ids_of, low_ref, high_ref):
    for block in range(low_ref.shape[0]):
        ids = ids_of(slice(block * LANES, (block + 1) * LANES))
        low_ref[block] = ids & (LOW - 1)
        high_ref[block] = ids // LOW


def start_kernel(
    coords_hbm, slice_hbm, history_hbm, message_ref, split_ref, low_ref, high_ref, coords_ref, ids_ref, history_ref, sems
):
    own, macros = ids_ref.shape
    offset = lax.axis_index("bunch") * own
    macro_total = macros * lax.axis_size("mp")
    copies = [pltpu.make_async_copy(coords_hbm.at[2 * plane], coords_ref.at[plane], sems.at[plane]) for plane in range(2)]
    copies.append(pltpu.make_async_copy(slice_hbm.at[0], ids_ref, sems.at[2]))
    copies.append(pltpu.make_async_copy(history_hbm, history_ref, sems.at[3]))
    for copy in copies:
        copy.start()
    centroids = []
    for plane in range(2):
        copies[plane].wait()
        sums = jnp.zeros((own, LANES), F32)
        for block in range(macros // LANES):
            piece = coords_ref[plane, :, block * LANES : (block + 1) * LANES]
            store_split(split_ref, plane, block, slice(None), piece)
            sums += piece
        centroids.append(jnp.sum(sums, axis=1, keepdims=True) / macro_total)
    copies[2].wait()
    store_digits(lambda span: ids_ref[:, span], low_ref, high_ref)
    copies[3].wait()
    rows, depth = history_ref.shape
    first = message_ref.shape[0] - rows
    store_centroids(message_ref.at[:first, :], centroids, offset)
    message_ref[first:, :] = jnp.concatenate([history_ref[...], jnp.zeros((rows, LANES - depth), F32)], axis=1)


def moments_kernel(split_ref, low_ref, high_ref, out_ref, block_ref):
    _, blocks, own, _ = split_ref.shape
    step = min(8, blocks)
    chunk = step * LANES
    low_levels = iota((LOW, chunk), 0)
    high_levels = iota((HIGH, chunk), 0)

    def one_bunch(bunch, carry):
        sums = jnp.zeros((5 * HIGH, LOW), F32)
        for start in range(0, blocks, step):

            def line(ref):
                rows = pl.ds(bunch, HIGH, stride=0)
                return jnp.concatenate([ref[start + block, rows, :] for block in range(step)], axis=1)

            ids = line(low_ref)
            low = jnp.concatenate([ids] * (LOW // HIGH), axis=0) == low_levels
            high = line(high_ref) == high_levels
            parts = [jnp.where(high, line(split_ref.at[part]), 0.0) for part in range(4)]
            parts.append(jnp.where(high, 1.0, 0.0))
            sums += lax.dot_general(
                jnp.concatenate(parts, axis=0).astype(BF16),
                low.astype(F32).astype(BF16),
                (((1,), (1,)), ((), ())),
                preferred_element_type=F32,
            )
        kinds = (sums[4 * HIGH :], sums[:HIGH] + sums[HIGH : 2 * HIGH], sums[2 * HIGH : 3 * HIGH] + sums[3 * HIGH : 4 * HIGH])
        for kind in range(3):
            block_ref[pl.ds(kind * HIGH * own + bunch, HIGH, stride=own), :] = kinds[kind]
        return carry

    lax.fori_loop(0, own, one_bunch, 0, unroll=True)
    each = LANES // LOW
    for kind in range(3):
        for half in range(HALVES):
            first = (kind * HIGH + half * each) * own
            out_ref[kind, half] = jnp.concatenate(
                [block_ref[first + level * own : first + (level + 1) * own, :] for level in range(each)], axis=1
            )


def prepare_kernel(depth, slice_ref, advance_ref, dipole_wake_ref, quad_wake_ref, wake_ref, *refs):
    history_refs = refs[:-6]
    low_ref, high_ref, turned_ref, wakes_ref, near_ref, older_ref = refs[-6:]
    own = slice_ref.shape[1]
    all_bunches = wake_ref.shape[1]
    shard = lax.axis_index("bunch")
    offset = shard * own
    store_digits(lambda span: slice_ref[1, :, span], low_ref, high_ref)
    for index, ref in enumerate((dipole_wake_ref, quad_wake_ref)):
        whole = ref[...]
        upper = whole.astype(BF16)
        wakes_ref[index, 0] = upper
        wakes_ref[index, 1] = (whole - upper.astype(F32)).astype(BF16)
    for plane in range(2):
        line = advance_ref[plane : plane + 1, :]
        for index, values in enumerate((jnp.sin(line), jnp.cos(line))):
            turned_ref[2 * plane + index] = jnp.broadcast_to(rows_to_column(values, 0, own), (own, LANES))
    lags = wake_rows(wake_ref[...])
    for turn in range(TURNS):
        for tile in range(near_ref.shape[1]):
            other = iota((own, LANES), 1) + tile * LANES
            index = all_bunches - 1 + offset + iota((own, LANES), 0) - other
            taken = gather_lanes(lags[turn : turn + 1], jnp.where(other < all_bunches, index, 0))
            near_ref[turn, tile] = jnp.where(other < all_bunches, taken, 0.0)
    ahead = [lags[1:]]
    for turn in range(1, TURNS):
        ahead.append(jnp.concatenate([lags[1 + turn :], jnp.zeros((turn, 2 * all_bunches), F32)], axis=0))
    history = jnp.concatenate([ref[-2 * own :, :depth] for ref in history_refs], axis=0)
    older = jnp.dot(history, jnp.concatenate(ahead, axis=1), precision=HIGHEST, preferred_element_type=F32)
    first_lane = iota((own, LANES), 1) == 0
    for turn in range(TURNS):
        span = slice(turn * 2 * all_bunches, (turn + 1) * 2 * all_bunches)
        for plane in range(2):
            row = total(
                [
                    spread_far(older[(2 * step + plane) * own : (2 * step + plane + 1) * own, span], (shard ^ step) * own)
                    for step in range(len(history_refs))
                ]
            )
            older_ref[turn, plane] = jnp.where(first_lane, rows_to_column(row, offset, own), 0.0)


def sincos(angle):
    turns = jnp.floor(angle * 0.3183098861837907 + 0.5)
    rest = angle - turns * 3.140625
    rest = rest - turns * 9.67502593994140625e-4
    rest = rest - turns * 1.509957990978376432e-7
    rest = jnp.clip(rest, -1.75, 1.75)
    square = rest * rest
    sine = -2.3889859e-8
    for term in (2.7525562e-6, -1.9840874e-4, 8.3333310e-3, -1.6666667e-1):
        sine = sine * square + term
    sine = rest + rest * (square * sine)
    cosine = -2.6051615e-7
    for term in (2.4760495e-5, -1.3888378e-3, 4.1666638e-2, -0.5):
        cosine = cosine * square + term
    cosine = 1.0 + square * cosine
    odd = (turns.astype(jnp.int32) & 1) != 0
    return jnp.where(odd, -sine, sine), jnp.where(odd, -cosine, cosine)


def wake_product(rows, wake_ref):
    contract = (((1,), (1,)), ((), ()))
    upper = rows.astype(BF16)
    lower = (rows - upper.astype(F32)).astype(BF16)
    both = jnp.concatenate([upper, lower], axis=0)
    count = rows.shape[0]
    first = lax.dot_general(both, wake_ref[0], contract, preferred_element_type=F32)
    second = lax.dot_general(upper, wake_ref[1], contract, preferred_element_type=F32)
    return first[:count] + first[count:] + second


def apply_kernel(last, coords_ref, slice_ref, mine_ref, other_ref, turned_ref, wakes_ref, near_ref, older_ref, *refs):
    turn = TURNS - 1 if last else 0
    _, own, macros = coords_ref.shape
    offset = lax.axis_index("bunch") * own
    macro_total = macros * lax.axis_size("mp")
    moment_rows = 3 * HALVES * own

    def both(first, count):
        return mine_ref[first : first + count, :] + other_ref[first : first + count, :]

    moments = [
        jnp.concatenate([both((kind * HALVES + half) * own, own) for half in range(HALVES)], axis=1) / macro_total
        for kind in range(3)
    ]
    small = [
        both(moment_rows + tile * SUBLANES, SUBLANES) for tile in range((mine_ref.shape[0] - moment_rows) // SUBLANES)
    ]
    if last:
        later_ref, earlier_centroid_ref, out_hbm_ref, centroid_ref, table_ref, out_ref, out_sem = refs
    else:
        out_ref, centroid_ref, later_ref, small_out_ref, split_ref, table_ref = refs

    def far_of(lag, plane):
        return total(
            [near_ref[lag, tile] * jnp.broadcast_to(part[plane : plane + 1], (own, LANES)) for tile, part in enumerate(small)]
        )

    far = []
    for plane in range(2):
        past = later_ref[plane] if last else older_ref[0, plane]
        far.append(jnp.sum(far_of(0, plane) + past, axis=1, keepdims=True))
    dip_kick = wake_product(jnp.concatenate(moments[1:], axis=0), wakes_ref.at[0])
    quad_kick = wake_product(moments[0], wakes_ref.at[1])
    for kind, table in enumerate((dip_kick[:own] + far[0], dip_kick[own:] + far[1], quad_kick)):
        for half in range(HALVES):
            table_ref[kind, half] = table[:, half * LANES : (half + 1) * LANES]
    centroid = jnp.concatenate(
        [column_to_row(jnp.sum(moments[1 + plane], axis=1, keepdims=True), 0, own) for plane in range(2)], axis=0
    )
    if last:
        for plane in range(2):
            centroid_ref[plane] = jnp.concatenate(
                [earlier_centroid_ref[plane : plane + 1], centroid[plane : plane + 1]], axis=0
            )
    else:
        centroid_ref[...] = centroid
        for plane in range(2):
            later_ref[plane] = far_of(1, plane) + older_ref[1, plane]

    chunk = min(1024, macros)
    parts, copies = [], []
    for group in range(0, own, SUBLANES):
        bunches = pl.ds(group, SUBLANES)
        tables = [[table_ref[kind, half, bunches, :] for half in range(HALVES)] for kind in range(3)]
        turned = [turned_ref[index, bunches, :] for index in range(4)]

        def step(index, sums):
            for start in range(0, chunk, LANES):
                span = pl.ds(index * chunk + start, LANES)
                ids = slice_ref[turn, bunches, span]
                within = ids & (LANES - 1)
                upper = ids >= LANES
                picked = [
                    jnp.where(
                        upper,
                        jnp.take_along_axis(table[1], within, axis=1),
                        jnp.take_along_axis(table[0], within, axis=1),
                    )
                    for table in tables
                ]
                x, mx, y, my = (coords_ref[row, bunches, span] for row in range(4))
                mx = mx + picked[0] + picked[2] * x
                my = my + picked[1] - picked[2] * y
                action = x * x + mx * mx + y * y + my * my
                sine, cosine = sincos(DETUNE * action)
                new_sums = []
                for plane, (u, v) in enumerate(((x, mx), (y, my))):
                    sine_0, cosine_0 = turned[2 * plane : 2 * plane + 2]
                    full_sine = sine_0 * cosine + cosine_0 * sine
                    full_cosine = cosine_0 * cosine - sine_0 * sine
                    new_u = full_cosine * u + full_sine * v
                    out_ref[2 * plane, bunches, span] = new_u
                    out_ref[2 * plane + 1, bunches, span] = full_cosine * v - full_sine * u
                    if not last:
                        store_split(split_ref, plane, index * (chunk // LANES) + start // LANES, bunches, new_u)
                        new_sums.append(sums[plane] + new_u)
                sums = tuple(new_sums)
            return sums

        zero = jnp.zeros((SUBLANES, LANES), F32)
        sums = () if last else (zero, zero)
        for index in range(macros // chunk):
            sums = step(index, sums)
            if last:
                area = (slice(None), bunches, pl.ds(index * chunk, chunk))
                copies.append(pltpu.make_async_copy(out_ref.at[area], out_hbm_ref.at[area], out_sem.at[len(copies)]))
                copies[-1].start()
        parts.append(sums)
    if last:
        for copy in copies:
            copy.wait()
        return
    store_centroids(
        small_out_ref,
        [
            jnp.sum(jnp.concatenate([part[plane] for part in parts], axis=0), axis=1, keepdims=True) / macro_total
            for plane in range(2)
        ],
        offset,
    )


VMEM = pl.BlockSpec(memory_space=pltpu.VMEM)
HBM = pl.BlockSpec(memory_space=pltpu.HBM)


def call(kernel, operands, outs, scratch=(), in_specs=None, out_specs=None, name=None):
    in_specs = in_specs or [VMEM] * len(operands)
    operands = [
        pltpu.with_memory_space_constraint(operand, pltpu.VMEM if spec is VMEM else pltpu.HBM)
        for operand, spec in zip(operands, in_specs)
    ]
    return pl.pallas_call(
        kernel,
        out_shape=outs,
        in_specs=in_specs,
        out_specs=out_specs or jax.tree.map(lambda out: VMEM, outs),
        scratch_shapes=list(scratch),
        compiler_params=pltpu.CompilerParams(vmem_limit_bytes=16 << 20),
        name=name,
    )(*operands)


def shape(dims, dtype=F32):
    return pltpu.VMEM(dims, dtype)


def over_bunches(value):
    size = lax.axis_size("bunch")
    return [value] + [
        lax.ppermute(value, "bunch", [(source, source ^ step) for source in range(size)]) for step in range(1, size)
    ]


def over_macros(value):
    size = lax.axis_size("mp")
    swap = [(source, source ^ 1) for source in range(size)]
    chip = value + lax.ppermute(value, "mp", swap)
    steps = list(range(size // CORES - 1, 0, -1))
    received = []
    for first in reversed(range(0, len(steps), CORES)):
        pairs = []
        for core, step in enumerate(steps[first : first + CORES]):
            pairs += [(source, source ^ (step * CORES)) for source in range(core, size, CORES)]
        received.append(lax.ppermute(chip, "mp", pairs))
    own = jnp.where(lax.axis_index("mp") % CORES == 0, chip, 0.0)
    mine = total([own] + received)
    return chip, mine, lax.ppermute(mine, "mp", swap)


def body(phase_space, phase_advance, centroid_history, lr_wake, sr_dipole, sr_quad, slice_ids):
    _, own, macros = phase_space.shape
    depth = centroid_history.shape[1]
    all_bunches = own * lax.axis_size("bunch")
    wake = lr_wake.reshape(depth + 1, all_bunches)
    history = centroid_history.transpose(0, 2, 1).reshape(2 * own, depth)
    tiles = pl.cdiv(all_bunches, LANES)
    small_rows = tiles * SUBLANES
    split_shape = shape((4, macros // LANES, own, LANES))
    digit_shape = shape((macros // LANES, own, LANES), jnp.int32)
    moment_rows = 3 * HALVES * own

    message, split, low, high = call(
        start_kernel,
        (phase_space, slice_ids, history),
        (shape((small_rows + 2 * own, LANES)), split_shape, digit_shape, digit_shape),
        [
            pltpu.VMEM((2, own, macros), F32),
            pltpu.VMEM((own, macros), jnp.int32),
            pltpu.VMEM(history.shape, F32),
            pltpu.SemaphoreType.DMA((4,)),
        ],
        [HBM, HBM, HBM],
        name="start",
    )
    coords = phase_space
    later = earlier_centroid = None
    for turn in range(TURNS):
        last = turn == TURNS - 1
        gathered = over_bunches(message)
        moments = call(
            moments_kernel,
            (split, low, high),
            shape((3, HALVES, own, LANES)),
            [pltpu.VMEM((3 * HIGH * own, LOW), F32)],
            name="moments",
        )
        small = total([part[:small_rows] for part in gathered])
        chip, mine, other = over_macros(jnp.concatenate([moments.reshape(moment_rows, LANES), small], axis=0))
        if turn == 0:
            low, high, turned, wakes, near, older = call(
                functools.partial(prepare_kernel, depth),
                [slice_ids, phase_advance, sr_dipole, sr_quad, wake] + gathered,
                (
                    digit_shape,
                    digit_shape,
                    shape((4, own, LANES)),
                    shape((2, 2, SLICES, SLICES), BF16),
                    shape((TURNS, tiles, own, LANES)),
                    shape((TURNS, 2, own, LANES)),
                ),
                name="prepare",
            )
        operands = (coords, slice_ids, mine, other, turned, wakes, near, older)
        table = pltpu.VMEM((3, HALVES, own, LANES), F32)
        if last:
            coords, centroids = call(
                functools.partial(apply_kernel, True),
                operands + (later, earlier_centroid),
                (jax.ShapeDtypeStruct(coords.shape, F32), jax.ShapeDtypeStruct((2, TURNS, own), F32)),
                [table, pltpu.VMEM(coords.shape, F32), pltpu.SemaphoreType.DMA((own // SUBLANES * pl.cdiv(macros, 1024),))],
                None,
                (HBM, VMEM),
                name="apply_last",
            )
        else:
            coords, earlier_centroid, later, message, split = call(
                functools.partial(apply_kernel, False),
                operands,
                (shape(coords.shape), shape((2, own)), shape((2, own, LANES)), shape((small_rows, LANES)), split_shape),
                [table],
                name="apply",
            )
    return coords, centroids


def solution(mesh):
    placed = (
        P(None, "bunch", "mp"),
        P(None, "bunch"),
        P(None, None, "bunch"),
        P(),
        P(),
        P(),
        P(None, "bunch", "mp"),
    )
    return jax.shard_map(
        body,
        mesh=mesh,
        in_specs=placed,
        out_specs=(P(None, "bunch", "mp"), P(None, None, "bunch")),
        check_vma=False,
    )
```

```python
import functools

import jax
import jax.numpy as jnp
from jax import lax
from jax.experimental import pallas as pl
from jax.experimental.pallas import tpu as pltpu
from jax.sharding import PartitionSpec as P

SLICES = 256
TURNS = 2
DETUNE = 0.02
LOW = 32
HIGH = SLICES // LOW
LANES = 128
SUBLANES = 8
HALVES = SLICES // LANES
CORES = 2
HIGHEST = lax.Precision.HIGHEST
F32 = jnp.float32
BF16 = jnp.bfloat16


def iota(shape, axis):
    return lax.broadcasted_iota(jnp.int32, shape, axis)


def total(values):
    return functools.reduce(lambda a, b: a + b, values)


def rows_to_column(row, offset, count):
    length = row.shape[1]
    pick = iota((count, length), 1) == iota((count, length), 0) + offset
    return jnp.sum(jnp.where(pick, jnp.broadcast_to(row, (count, length)), 0.0), axis=1, keepdims=True)


def column_to_row(column, offset, length):
    count = column.shape[0]
    pick = iota((count, length), 1) == iota((count, length), 0) + offset
    return jnp.sum(jnp.where(pick, jnp.broadcast_to(column, (count, length)), 0.0), axis=0, keepdims=True)


def spread_far(weighted, offset):
    own, width = weighted.shape
    rows = iota((own, width), 0)
    step = 1
    while step < own:
        weighted = jnp.where((rows & step) != 0, pltpu.roll(weighted, step, 1), weighted)
        step *= 2
    return pltpu.roll(jnp.sum(weighted, axis=0, keepdims=True), width // 2 + 1 + offset, 1)


def gather_lanes(row, index):
    count = index.shape[0]
    result = jnp.zeros(index.shape, F32)
    for tile in range(row.shape[1] // LANES):
        part = jnp.broadcast_to(row[:, tile * LANES : (tile + 1) * LANES], (count, LANES))
        taken = jnp.take_along_axis(part, index & (LANES - 1), axis=1)
        result = jnp.where(index // LANES == tile, taken, result)
    return result


def store_centroids(small_ref, columns, offset):
    tiles = small_ref.shape[0] // SUBLANES
    rows = [column_to_row(column, offset, tiles * LANES) for column in columns]
    rows.append(jnp.zeros((SUBLANES - len(rows), tiles * LANES), F32))
    whole = jnp.concatenate(rows, axis=0)
    for tile in range(tiles):
        small_ref[tile * SUBLANES : (tile + 1) * SUBLANES, :] = whole[:, tile * LANES : (tile + 1) * LANES]


def wake_rows(wake):
    before = jnp.concatenate([jnp.zeros((1, wake.shape[1]), F32), wake[:-1]], axis=0)
    return jnp.concatenate([before, wake], axis=1)


def store_split(split_ref, plane, block, bunches, values):
    upper = values.astype(BF16).astype(F32)
    split_ref[2 * plane, block, bunches, :] = upper
    split_ref[2 * plane + 1, block, bunches, :] = values - upper


def store_digits(ids_of, low_ref, high_ref):
    for block in range(low_ref.shape[0]):
        ids = ids_of(slice(block * LANES, (block + 1) * LANES))
        low_ref[block] = ids & (LOW - 1)
        high_ref[block] = ids // LOW


def start_kernel(
    coords_hbm, slice_hbm, history_hbm, message_ref, split_ref, low_ref, high_ref, coords_ref, ids_ref, history_ref, sems
):
    own, macros = ids_ref.shape
    offset = lax.axis_index("bunch") * own
    macro_total = macros * lax.axis_size("mp")
    copies = [pltpu.make_async_copy(coords_hbm.at[2 * plane], coords_ref.at[plane], sems.at[plane]) for plane in range(2)]
    copies.append(pltpu.make_async_copy(slice_hbm.at[0], ids_ref, sems.at[2]))
    copies.append(pltpu.make_async_copy(history_hbm, history_ref, sems.at[3]))
    for copy in copies:
        copy.start()
    centroids = []
    for plane in range(2):
        copies[plane].wait()
        sums = jnp.zeros((own, LANES), F32)
        for block in range(macros // LANES):
            piece = coords_ref[plane, :, block * LANES : (block + 1) * LANES]
            store_split(split_ref, plane, block, slice(None), piece)
            sums += piece
        centroids.append(jnp.sum(sums, axis=1, keepdims=True) / macro_total)
    copies[2].wait()
    store_digits(lambda span: ids_ref[:, span], low_ref, high_ref)
    copies[3].wait()
    rows, depth = history_ref.shape
    first = message_ref.shape[0] - rows
    store_centroids(message_ref.at[:first, :], centroids, offset)
    message_ref[first:, :] = jnp.concatenate([history_ref[...], jnp.zeros((rows, LANES - depth), F32)], axis=1)


def moments_kernel(split_ref, low_ref, high_ref, out_ref, block_ref):
    _, blocks, own, _ = split_ref.shape
    step = min(8, blocks)
    chunk = step * LANES
    low_levels = iota((LOW, chunk), 0)
    high_levels = iota((HIGH, chunk), 0)

    def one_bunch(bunch, carry):
        sums = jnp.zeros((5 * HIGH, LOW), F32)
        for start in range(0, blocks, step):

            def line(ref):
                rows = pl.ds(bunch, HIGH, stride=0)
                return jnp.concatenate([ref[start + block, rows, :] for block in range(step)], axis=1)

            ids = line(low_ref)
            low = jnp.concatenate([ids] * (LOW // HIGH), axis=0) == low_levels
            high = line(high_ref) == high_levels
            parts = [jnp.where(high, line(split_ref.at[part]), 0.0) for part in range(4)]
            parts.append(jnp.where(high, 1.0, 0.0))
            sums += lax.dot_general(
                jnp.concatenate(parts, axis=0).astype(BF16),
                low.astype(F32).astype(BF16),
                (((1,), (1,)), ((), ())),
                preferred_element_type=F32,
            )
        kinds = (sums[4 * HIGH :], sums[:HIGH] + sums[HIGH : 2 * HIGH], sums[2 * HIGH : 3 * HIGH] + sums[3 * HIGH : 4 * HIGH])
        for kind in range(3):
            block_ref[pl.ds(kind * HIGH * own + bunch, HIGH, stride=own), :] = kinds[kind]
        return carry

    lax.fori_loop(0, own, one_bunch, 0, unroll=True)
    each = LANES // LOW
    for kind in range(3):
        for half in range(HALVES):
            first = (kind * HIGH + half * each) * own
            out_ref[kind, half] = jnp.concatenate(
                [block_ref[first + level * own : first + (level + 1) * own, :] for level in range(each)], axis=1
            )


def prepare_kernel(depth, slice_ref, advance_ref, dipole_wake_ref, quad_wake_ref, wake_ref, *refs):
    history_refs = refs[:-6]
    low_ref, high_ref, turned_ref, wakes_ref, near_ref, older_ref = refs[-6:]
    own = slice_ref.shape[1]
    all_bunches = wake_ref.shape[1]
    shard = lax.axis_index("bunch")
    offset = shard * own
    store_digits(lambda span: slice_ref[1, :, span], low_ref, high_ref)
    for index, ref in enumerate((dipole_wake_ref, quad_wake_ref)):
        whole = ref[...]
        upper = whole.astype(BF16)
        wakes_ref[index, 0] = upper
        wakes_ref[index, 1] = (whole - upper.astype(F32)).astype(BF16)
    for plane in range(2):
        line = advance_ref[plane : plane + 1, :]
        for index, values in enumerate((jnp.sin(line), jnp.cos(line))):
            turned_ref[2 * plane + index] = jnp.broadcast_to(rows_to_column(values, 0, own), (own, LANES))
    lags = wake_rows(wake_ref[...])
    for turn in range(TURNS):
        for tile in range(near_ref.shape[1]):
            other = iota((own, LANES), 1) + tile * LANES
            index = all_bunches - 1 + offset + iota((own, LANES), 0) - other
            taken = gather_lanes(lags[turn : turn + 1], jnp.where(other < all_bunches, index, 0))
            near_ref[turn, tile] = jnp.where(other < all_bunches, taken, 0.0)
    ahead = [lags[1:]]
    for turn in range(1, TURNS):
        ahead.append(jnp.concatenate([lags[1 + turn :], jnp.zeros((turn, 2 * all_bunches), F32)], axis=0))
    history = jnp.concatenate([ref[-2 * own :, :depth] for ref in history_refs], axis=0)
    older = jnp.dot(history, jnp.concatenate(ahead, axis=1), precision=HIGHEST, preferred_element_type=F32)
    first_lane = iota((own, LANES), 1) == 0
    for turn in range(TURNS):
        span = slice(turn * 2 * all_bunches, (turn + 1) * 2 * all_bunches)
        for plane in range(2):
            row = total(
                [
                    spread_far(older[(2 * step + plane) * own : (2 * step + plane + 1) * own, span], (shard ^ step) * own)
                    for step in range(len(history_refs))
                ]
            )
            older_ref[turn, plane] = jnp.where(first_lane, rows_to_column(row, offset, own), 0.0)


def sincos(angle):
    turns = jnp.floor(angle * 0.3183098861837907 + 0.5)
    rest = angle - turns * 3.140625
    rest = rest - turns * 9.67502593994140625e-4
    rest = rest - turns * 1.509957990978376432e-7
    rest = jnp.clip(rest, -1.75, 1.75)
    square = rest * rest
    sine = -2.3889859e-8
    for term in (2.7525562e-6, -1.9840874e-4, 8.3333310e-3, -1.6666667e-1):
        sine = sine * square + term
    sine = rest + rest * (square * sine)
    cosine = -2.6051615e-7
    for term in (2.4760495e-5, -1.3888378e-3, 4.1666638e-2, -0.5):
        cosine = cosine * square + term
    cosine = 1.0 + square * cosine
    odd = (turns.astype(jnp.int32) & 1) != 0
    return jnp.where(odd, -sine, sine), jnp.where(odd, -cosine, cosine)


def wake_product(rows, wake_ref):
    contract = (((1,), (1,)), ((), ()))
    upper = rows.astype(BF16)
    lower = (rows - upper.astype(F32)).astype(BF16)
    both = jnp.concatenate([upper, lower], axis=0)
    count = rows.shape[0]
    first = lax.dot_general(both, wake_ref[0], contract, preferred_element_type=F32)
    second = lax.dot_general(upper, wake_ref[1], contract, preferred_element_type=F32)
    return first[:count] + first[count:] + second


def apply_kernel(last, coords_ref, slice_ref, mine_ref, other_ref, turned_ref, wakes_ref, near_ref, older_ref, *refs):
    turn = TURNS - 1 if last else 0
    _, own, macros = coords_ref.shape
    offset = lax.axis_index("bunch") * own
    macro_total = macros * lax.axis_size("mp")
    moment_rows = 3 * HALVES * own

    def both(first, count):
        return mine_ref[first : first + count, :] + other_ref[first : first + count, :]

    moments = [
        jnp.concatenate([both((kind * HALVES + half) * own, own) for half in range(HALVES)], axis=1) / macro_total
        for kind in range(3)
    ]
    small = [
        both(moment_rows + tile * SUBLANES, SUBLANES) for tile in range((mine_ref.shape[0] - moment_rows) // SUBLANES)
    ]
    if last:
        later_ref, earlier_centroid_ref, out_hbm_ref, centroid_ref, table_ref, out_ref, out_sem = refs
    else:
        out_ref, centroid_ref, later_ref, small_out_ref, split_ref, table_ref = refs

    def far_of(lag, plane):
        return total(
            [near_ref[lag, tile] * jnp.broadcast_to(part[plane : plane + 1], (own, LANES)) for tile, part in enumerate(small)]
        )

    far = []
    for plane in range(2):
        past = later_ref[plane] if last else older_ref[0, plane]
        far.append(jnp.sum(far_of(0, plane) + past, axis=1, keepdims=True))
    dip_kick = wake_product(jnp.concatenate(moments[1:], axis=0), wakes_ref.at[0])
    quad_kick = wake_product(moments[0], wakes_ref.at[1])
    for kind, table in enumerate((dip_kick[:own] + far[0], dip_kick[own:] + far[1], quad_kick)):
        for half in range(HALVES):
            table_ref[kind, half] = table[:, half * LANES : (half + 1) * LANES]
    centroid = jnp.concatenate(
        [column_to_row(jnp.sum(moments[1 + plane], axis=1, keepdims=True), 0, own) for plane in range(2)], axis=0
    )
    if last:
        for plane in range(2):
            centroid_ref[plane] = jnp.concatenate(
                [earlier_centroid_ref[plane : plane + 1], centroid[plane : plane + 1]], axis=0
            )
    else:
        centroid_ref[...] = centroid
        for plane in range(2):
            later_ref[plane] = far_of(1, plane) + older_ref[1, plane]

    chunk = min(1024, macros)
    parts, copies = [], []
    for group in range(0, own, SUBLANES):
        bunches = pl.ds(group, SUBLANES)
        tables = [[table_ref[kind, half, bunches, :] for half in range(HALVES)] for kind in range(3)]
        turned = [turned_ref[index, bunches, :] for index in range(4)]

        def step(index, sums):
            for start in range(0, chunk, LANES):
                span = pl.ds(index * chunk + start, LANES)
                ids = slice_ref[turn, bunches, span]
                within = ids & (LANES - 1)
                upper = ids >= LANES
                picked = [
                    jnp.where(
                        upper,
                        jnp.take_along_axis(table[1], within, axis=1),
                        jnp.take_along_axis(table[0], within, axis=1),
                    )
                    for table in tables
                ]
                x, mx, y, my = (coords_ref[row, bunches, span] for row in range(4))
                mx = mx + picked[0] + picked[2] * x
                my = my + picked[1] - picked[2] * y
                action = x * x + mx * mx + y * y + my * my
                sine, cosine = sincos(DETUNE * action)
                new_sums = []
                for plane, (u, v) in enumerate(((x, mx), (y, my))):
                    sine_0, cosine_0 = turned[2 * plane : 2 * plane + 2]
                    full_sine = sine_0 * cosine + cosine_0 * sine
                    full_cosine = cosine_0 * cosine - sine_0 * sine
                    new_u = full_cosine * u + full_sine * v
                    out_ref[2 * plane, bunches, span] = new_u
                    out_ref[2 * plane + 1, bunches, span] = full_cosine * v - full_sine * u
                    if not last:
                        store_split(split_ref, plane, index * (chunk // LANES) + start // LANES, bunches, new_u)
                        new_sums.append(sums[plane] + new_u)
                sums = tuple(new_sums)
            return sums

        zero = jnp.zeros((SUBLANES, LANES), F32)
        sums = () if last else (zero, zero)
        for index in range(macros // chunk):
            sums = step(index, sums)
            if last:
                area = (slice(None), bunches, pl.ds(index * chunk, chunk))
                copies.append(pltpu.make_async_copy(out_ref.at[area], out_hbm_ref.at[area], out_sem.at[len(copies)]))
                copies[-1].start()
        parts.append(sums)
    if last:
        for copy in copies:
            copy.wait()
        return
    store_centroids(
        small_out_ref,
        [
            jnp.sum(jnp.concatenate([part[plane] for part in parts], axis=0), axis=1, keepdims=True) / macro_total
            for plane in range(2)
        ],
        offset,
    )


VMEM = pl.BlockSpec(memory_space=pltpu.VMEM)
HBM = pl.BlockSpec(memory_space=pltpu.HBM)


def call(kernel, operands, outs, scratch=(), in_specs=None, out_specs=None, name=None):
    in_specs = in_specs or [VMEM] * len(operands)
    operands = [
        pltpu.with_memory_space_constraint(operand, pltpu.VMEM if spec is VMEM else pltpu.HBM)
        for operand, spec in zip(operands, in_specs)
    ]
    return pl.pallas_call(
        kernel,
        out_shape=outs,
        in_specs=in_specs,
        out_specs=out_specs or jax.tree.map(lambda out: VMEM, outs),
        scratch_shapes=list(scratch),
        compiler_params=pltpu.CompilerParams(vmem_limit_bytes=16 << 20),
        name=name,
    )(*operands)


def shape(dims, dtype=F32):
    return pltpu.VMEM(dims, dtype)


def swap_cores(value):
    return lax.ppermute(value, "mp", [(source, source ^ 1) for source in range(lax.axis_size("mp"))])


def over_bunches(value):
    size, inner = lax.axis_size("bunch"), lax.axis_size("mp")
    return [value] + [
        lax.ppermute(value, ("bunch", "mp"), [(source, (source ^ (step * inner)) ^ 1) for source in range(size * inner)])
        for step in range(1, size)
    ]


def over_macros(value):
    size = lax.axis_size("mp")
    chip = value + swap_cores(value)
    core = lax.axis_index("mp") % CORES
    steps = list(range(size // CORES - 1, 0, -1))
    received = []
    for first in reversed(range(0, len(steps), CORES)):
        taken = steps[first : first + CORES]
        hop = [taken[min(core_from, len(taken) - 1)] * CORES for core_from in range(CORES)]
        part = lax.ppermute(chip, "mp", [(source, (source ^ hop[source % CORES]) ^ 1) for source in range(size)])
        received.append(part if len(taken) == CORES else jnp.where(core == 0, part, 0.0))
    mine = total([jnp.where(core == 0, chip, 0.0)] + received)
    return mine, swap_cores(mine)


def body(phase_space, phase_advance, centroid_history, lr_wake, sr_dipole, sr_quad, slice_ids):
    _, own, macros = phase_space.shape
    depth = centroid_history.shape[1]
    all_bunches = own * lax.axis_size("bunch")
    wake = lr_wake.reshape(depth + 1, all_bunches)
    history = centroid_history.transpose(0, 2, 1).reshape(2 * own, depth)
    tiles = pl.cdiv(all_bunches, LANES)
    small_rows = tiles * SUBLANES
    split_shape = shape((4, macros // LANES, own, LANES))
    digit_shape = shape((macros // LANES, own, LANES), jnp.int32)
    moment_rows = 3 * HALVES * own

    message, split, low, high = call(
        start_kernel,
        (phase_space, slice_ids, history),
        (shape((small_rows + 2 * own, LANES)), split_shape, digit_shape, digit_shape),
        [
            pltpu.VMEM((2, own, macros), F32),
            pltpu.VMEM((own, macros), jnp.int32),
            pltpu.VMEM(history.shape, F32),
            pltpu.SemaphoreType.DMA((4,)),
        ],
        [HBM, HBM, HBM],
        name="start",
    )
    coords = phase_space
    later = earlier_centroid = None
    for turn in range(TURNS):
        last = turn == TURNS - 1
        gathered = over_bunches(message)
        moments = call(
            moments_kernel,
            (split, low, high),
            shape((3, HALVES, own, LANES)),
            [pltpu.VMEM((3 * HIGH * own, LOW), F32)],
            name="moments",
        )
        small = total([part[:small_rows] for part in gathered])
        mine, other = over_macros(jnp.concatenate([moments.reshape(moment_rows, LANES), small], axis=0))
        if turn == 0:
            low, high, turned, wakes, near, older = call(
                functools.partial(prepare_kernel, depth),
                [slice_ids, phase_advance, sr_dipole, sr_quad, wake] + gathered,
                (
                    digit_shape,
                    digit_shape,
                    shape((4, own, LANES)),
                    shape((2, 2, SLICES, SLICES), BF16),
                    shape((TURNS, tiles, own, LANES)),
                    shape((TURNS, 2, own, LANES)),
                ),
                name="prepare",
            )
        operands = (coords, slice_ids, mine, other, turned, wakes, near, older)
        table = pltpu.VMEM((3, HALVES, own, LANES), F32)
        if last:
            coords, centroids = call(
                functools.partial(apply_kernel, True),
                operands + (later, earlier_centroid),
                (jax.ShapeDtypeStruct(coords.shape, F32), jax.ShapeDtypeStruct((2, TURNS, own), F32)),
                [table, pltpu.VMEM(coords.shape, F32), pltpu.SemaphoreType.DMA((own // SUBLANES * pl.cdiv(macros, 1024),))],
                None,
                (HBM, VMEM),
                name="apply_last",
            )
        else:
            coords, earlier_centroid, later, message, split = call(
                functools.partial(apply_kernel, False),
                operands,
                (shape(coords.shape), shape((2, own)), shape((2, own, LANES)), shape((small_rows, LANES)), split_shape),
                [table],
                name="apply",
            )
    return coords, centroids


def solution(mesh):
    placed = (
        P(None, "bunch", "mp"),
        P(None, "bunch"),
        P(None, None, "bunch"),
        P(),
        P(),
        P(),
        P(None, "bunch", "mp"),
    )
    return jax.shard_map(
        body,
        mesh=mesh,
        in_specs=placed,
        out_specs=(P(None, "bunch", "mp"), P(None, None, "bunch")),
        check_vma=False,
    )
```

```python
import functools

import jax
import jax.numpy as jnp
from jax import lax
from jax.experimental import pallas as pl
from jax.experimental.pallas import tpu as pltpu
from jax.sharding import PartitionSpec as P

SLICES = 256
TURNS = 2
DETUNE = 0.02
LOW = 32
HIGH = SLICES // LOW
LANES = 128
SUBLANES = 8
HALVES = SLICES // LANES
CORES = 2
HIGHEST = lax.Precision.HIGHEST
F32 = jnp.float32
BF16 = jnp.bfloat16


def iota(shape, axis):
    return lax.broadcasted_iota(jnp.int32, shape, axis)


def total(values):
    return functools.reduce(lambda a, b: a + b, values)


def rows_to_column(row, offset, count):
    length = row.shape[1]
    pick = iota((count, length), 1) == iota((count, length), 0) + offset
    return jnp.sum(jnp.where(pick, jnp.broadcast_to(row, (count, length)), 0.0), axis=1, keepdims=True)


def column_to_row(column, offset, length):
    count = column.shape[0]
    pick = iota((count, length), 1) == iota((count, length), 0) + offset
    return jnp.sum(jnp.where(pick, jnp.broadcast_to(column, (count, length)), 0.0), axis=0, keepdims=True)


def spread_far(weighted, offset):
    own, width = weighted.shape
    rows = iota((own, width), 0)
    step = 1
    while step < own:
        weighted = jnp.where((rows & step) != 0, pltpu.roll(weighted, step, 1), weighted)
        step *= 2
    return pltpu.roll(jnp.sum(weighted, axis=0, keepdims=True), width // 2 + 1 + offset, 1)


def gather_lanes(row, index):
    count = index.shape[0]
    result = jnp.zeros(index.shape, F32)
    for tile in range(row.shape[1] // LANES):
        part = jnp.broadcast_to(row[:, tile * LANES : (tile + 1) * LANES], (count, LANES))
        taken = jnp.take_along_axis(part, index & (LANES - 1), axis=1)
        result = jnp.where(index // LANES == tile, taken, result)
    return result


def store_centroids(small_ref, columns, offset):
    tiles = small_ref.shape[0] // SUBLANES
    rows = [column_to_row(column, offset, tiles * LANES) for column in columns]
    rows.append(jnp.zeros((SUBLANES - len(rows), tiles * LANES), F32))
    whole = jnp.concatenate(rows, axis=0)
    for tile in range(tiles):
        small_ref[tile * SUBLANES : (tile + 1) * SUBLANES, :] = whole[:, tile * LANES : (tile + 1) * LANES]


def wake_rows(wake):
    before = jnp.concatenate([jnp.zeros((1, wake.shape[1]), F32), wake[:-1]], axis=0)
    return jnp.concatenate([before, wake], axis=1)


def store_split(split_ref, plane, block, bunches, values):
    upper = values.astype(BF16).astype(F32)
    split_ref[2 * plane, block, bunches, :] = upper
    split_ref[2 * plane + 1, block, bunches, :] = values - upper


def store_digits(ids_of, low_ref, high_ref):
    for block in range(low_ref.shape[0]):
        ids = ids_of(slice(block * LANES, (block + 1) * LANES))
        low_ref[block] = ids & (LOW - 1)
        high_ref[block] = ids // LOW


def start_kernel(
    coords_hbm, slice_hbm, history_hbm, message_ref, split_ref, low_ref, high_ref, coords_ref, ids_ref, history_ref, sems
):
    own, macros = ids_ref.shape
    offset = lax.axis_index("bunch") * own
    macro_total = macros * lax.axis_size("mp")
    copies = [pltpu.make_async_copy(coords_hbm.at[2 * plane], coords_ref.at[plane], sems.at[plane]) for plane in range(2)]
    copies.append(pltpu.make_async_copy(slice_hbm.at[0], ids_ref, sems.at[2]))
    copies.append(pltpu.make_async_copy(history_hbm, history_ref, sems.at[3]))
    for copy in copies:
        copy.start()
    centroids = []
    for plane in range(2):
        copies[plane].wait()
        sums = jnp.zeros((own, LANES), F32)
        for block in range(macros // LANES):
            piece = coords_ref[plane, :, block * LANES : (block + 1) * LANES]
            store_split(split_ref, plane, block, slice(None), piece)
            sums += piece
        centroids.append(jnp.sum(sums, axis=1, keepdims=True) / macro_total)
    copies[2].wait()
    store_digits(lambda span: ids_ref[:, span], low_ref, high_ref)
    copies[3].wait()
    rows, depth = history_ref.shape
    first = message_ref.shape[0] - rows
    store_centroids(message_ref.at[:first, :], centroids, offset)
    message_ref[first:, :] = jnp.concatenate([history_ref[...], jnp.zeros((rows, LANES - depth), F32)], axis=1)


def moments_kernel(split_ref, low_ref, high_ref, out_ref, block_ref):
    _, blocks, own, _ = split_ref.shape
    step = min(8, blocks)
    chunk = step * LANES
    low_levels = iota((LOW, chunk), 0)
    high_levels = iota((HIGH, chunk), 0)

    def one_bunch(bunch, carry):
        sums = jnp.zeros((5 * HIGH, LOW), F32)
        for start in range(0, blocks, step):

            def line(ref):
                rows = pl.ds(bunch, HIGH, stride=0)
                return jnp.concatenate([ref[start + block, rows, :] for block in range(step)], axis=1)

            ids = line(low_ref)
            low = jnp.concatenate([ids] * (LOW // HIGH), axis=0) == low_levels
            high = line(high_ref) == high_levels
            parts = [jnp.where(high, line(split_ref.at[part]), 0.0) for part in range(4)]
            parts.append(jnp.where(high, 1.0, 0.0))
            sums += lax.dot_general(
                jnp.concatenate(parts, axis=0).astype(BF16),
                low.astype(F32).astype(BF16),
                (((1,), (1,)), ((), ())),
                preferred_element_type=F32,
            )
        kinds = (sums[4 * HIGH :], sums[:HIGH] + sums[HIGH : 2 * HIGH], sums[2 * HIGH : 3 * HIGH] + sums[3 * HIGH : 4 * HIGH])
        for kind in range(3):
            block_ref[pl.ds(kind * HIGH * own + bunch, HIGH, stride=own), :] = kinds[kind]
        return carry

    lax.fori_loop(0, own, one_bunch, 0, unroll=True)
    each = LANES // LOW
    for kind in range(3):
        for half in range(HALVES):
            first = (kind * HIGH + half * each) * own
            out_ref[kind, half] = jnp.concatenate(
                [block_ref[first + level * own : first + (level + 1) * own, :] for level in range(each)], axis=1
            )


def prepare_kernel(depth, slice_ref, advance_ref, dipole_wake_ref, quad_wake_ref, wake_ref, *refs):
    history_refs = refs[:-6]
    low_ref, high_ref, turned_ref, wakes_ref, near_ref, older_ref = refs[-6:]
    own = slice_ref.shape[1]
    all_bunches = wake_ref.shape[1]
    shard = lax.axis_index("bunch")
    offset = shard * own
    store_digits(lambda span: slice_ref[1, :, span], low_ref, high_ref)
    for index, ref in enumerate((dipole_wake_ref, quad_wake_ref)):
        whole = ref[...]
        upper = whole.astype(BF16)
        wakes_ref[index, 0] = upper
        wakes_ref[index, 1] = (whole - upper.astype(F32)).astype(BF16)
    for plane in range(2):
        line = advance_ref[plane : plane + 1, :]
        for index, values in enumerate((jnp.sin(line), jnp.cos(line))):
            turned_ref[2 * plane + index] = jnp.broadcast_to(rows_to_column(values, 0, own), (own, LANES))
    lags = wake_rows(wake_ref[...])
    for turn in range(TURNS):
        for tile in range(near_ref.shape[1]):
            other = iota((own, LANES), 1) + tile * LANES
            index = all_bunches - 1 + offset + iota((own, LANES), 0) - other
            taken = gather_lanes(lags[turn : turn + 1], jnp.where(other < all_bunches, index, 0))
            near_ref[turn, tile] = jnp.where(other < all_bunches, taken, 0.0)
    ahead = [lags[1:]]
    for turn in range(1, TURNS):
        ahead.append(jnp.concatenate([lags[1 + turn :], jnp.zeros((turn, 2 * all_bunches), F32)], axis=0))
    history = jnp.concatenate([ref[-2 * own :, :depth] for ref in history_refs], axis=0)
    older = jnp.dot(history, jnp.concatenate(ahead, axis=1), precision=HIGHEST, preferred_element_type=F32)
    first_lane = iota((own, LANES), 1) == 0
    for turn in range(TURNS):
        span = slice(turn * 2 * all_bunches, (turn + 1) * 2 * all_bunches)
        for plane in range(2):
            row = total(
                [
                    spread_far(older[(2 * step + plane) * own : (2 * step + plane + 1) * own, span], (shard ^ step) * own)
                    for step in range(len(history_refs))
                ]
            )
            older_ref[turn, plane] = jnp.where(first_lane, rows_to_column(row, offset, own), 0.0)


def sincos(angle):
    turns = jnp.floor(angle * 0.3183098861837907 + 0.5)
    rest = angle - turns * 3.140625
    rest = rest - turns * 9.67502593994140625e-4
    rest = rest - turns * 1.509957990978376432e-7
    rest = jnp.clip(rest, -1.75, 1.75)
    square = rest * rest
    sine = -2.3889859e-8
    for term in (2.7525562e-6, -1.9840874e-4, 8.3333310e-3, -1.6666667e-1):
        sine = sine * square + term
    sine = rest + rest * (square * sine)
    cosine = -2.6051615e-7
    for term in (2.4760495e-5, -1.3888378e-3, 4.1666638e-2, -0.5):
        cosine = cosine * square + term
    cosine = 1.0 + square * cosine
    half = turns * 0.5
    sign = jnp.where(half == jnp.floor(half), 1.0, -1.0)
    return sign * sine, sign * cosine


def wake_product(rows, wake_ref):
    contract = (((1,), (1,)), ((), ()))
    upper = rows.astype(BF16)
    lower = (rows - upper.astype(F32)).astype(BF16)
    both = jnp.concatenate([upper, lower], axis=0)
    count = rows.shape[0]
    first = lax.dot_general(both, wake_ref[0], contract, preferred_element_type=F32)
    second = lax.dot_general(upper, wake_ref[1], contract, preferred_element_type=F32)
    return first[:count] + first[count:] + second


def apply_kernel(last, coords_ref, slice_ref, mine_ref, other_ref, turned_ref, wakes_ref, near_ref, older_ref, *refs):
    turn = TURNS - 1 if last else 0
    _, own, macros = coords_ref.shape
    offset = lax.axis_index("bunch") * own
    macro_total = macros * lax.axis_size("mp")
    moment_rows = 3 * HALVES * own

    def both(first, count):
        return mine_ref[first : first + count, :] + other_ref[first : first + count, :]

    moments = [
        jnp.concatenate([both((kind * HALVES + half) * own, own) for half in range(HALVES)], axis=1) / macro_total
        for kind in range(3)
    ]
    small = [
        both(moment_rows + tile * SUBLANES, SUBLANES) for tile in range((mine_ref.shape[0] - moment_rows) // SUBLANES)
    ]
    if last:
        later_ref, earlier_centroid_ref, out_hbm_ref, centroid_hbm_ref, table_ref, out_ref, centroid_ref, out_sem = refs
    else:
        out_ref, centroid_ref, later_ref, small_out_ref, split_ref, table_ref = refs

    copies = []

    def far_of(lag, plane):
        return total(
            [near_ref[lag, tile] * jnp.broadcast_to(part[plane : plane + 1], (own, LANES)) for tile, part in enumerate(small)]
        )

    far = []
    for plane in range(2):
        past = later_ref[plane] if last else older_ref[0, plane]
        far.append(jnp.sum(far_of(0, plane) + past, axis=1, keepdims=True))
    dip_kick = wake_product(jnp.concatenate(moments[1:], axis=0), wakes_ref.at[0])
    quad_kick = wake_product(moments[0], wakes_ref.at[1])
    for kind, table in enumerate((dip_kick[:own] + far[0], dip_kick[own:] + far[1], quad_kick)):
        for half in range(HALVES):
            table_ref[kind, half] = table[:, half * LANES : (half + 1) * LANES]
    centroid = jnp.concatenate(
        [column_to_row(jnp.sum(moments[1 + plane], axis=1, keepdims=True), 0, own) for plane in range(2)], axis=0
    )
    if last:
        for plane in range(2):
            centroid_ref[plane] = jnp.concatenate(
                [earlier_centroid_ref[plane : plane + 1], centroid[plane : plane + 1]], axis=0
            )
        copies.append(pltpu.make_async_copy(centroid_ref, centroid_hbm_ref, out_sem.at[0]))
        copies[-1].start()
    else:
        centroid_ref[...] = centroid
        for plane in range(2):
            later_ref[plane] = far_of(1, plane) + older_ref[1, plane]

    chunk = min(1024, macros)
    parts = []
    for group in range(0, own, SUBLANES):
        bunches = pl.ds(group, SUBLANES)
        tables = [[table_ref[kind, half, bunches, :] for half in range(HALVES)] for kind in range(3)]
        turned = [turned_ref[index, bunches, :] for index in range(4)]

        def step(index, sums):
            for start in range(0, chunk, LANES):
                span = pl.ds(index * chunk + start, LANES)
                ids = slice_ref[turn, bunches, span]
                within = ids & (LANES - 1)
                upper = ids >= LANES
                picked = [
                    jnp.where(
                        upper,
                        jnp.take_along_axis(table[1], within, axis=1, mode="promise_in_bounds"),
                        jnp.take_along_axis(table[0], within, axis=1, mode="promise_in_bounds"),
                    )
                    for table in tables
                ]
                x, mx, y, my = (coords_ref[row, bunches, span] for row in range(4))
                mx = mx + picked[0] + picked[2] * x
                my = my + picked[1] - picked[2] * y
                action = x * x + mx * mx + y * y + my * my
                sine, cosine = sincos(DETUNE * action)
                new_sums = []
                for plane, (u, v) in enumerate(((x, mx), (y, my))):
                    sine_0, cosine_0 = turned[2 * plane : 2 * plane + 2]
                    full_sine = sine_0 * cosine + cosine_0 * sine
                    full_cosine = cosine_0 * cosine - sine_0 * sine
                    new_u = full_cosine * u + full_sine * v
                    out_ref[2 * plane, bunches, span] = new_u
                    out_ref[2 * plane + 1, bunches, span] = full_cosine * v - full_sine * u
                    if not last:
                        store_split(split_ref, plane, index * (chunk // LANES) + start // LANES, bunches, new_u)
                        new_sums.append(sums[plane] + new_u)
                sums = tuple(new_sums)
            return sums

        zero = jnp.zeros((SUBLANES, LANES), F32)
        sums = () if last else (zero, zero)
        for index in range(macros // chunk):
            sums = step(index, sums)
            if last:
                area = (slice(None), bunches, pl.ds(index * chunk, chunk))
                copies.append(pltpu.make_async_copy(out_ref.at[area], out_hbm_ref.at[area], out_sem.at[len(copies)]))
                copies[-1].start()
        parts.append(sums)
    if last:
        for copy in copies:
            copy.wait()
        return
    store_centroids(
        small_out_ref,
        [
            jnp.sum(jnp.concatenate([part[plane] for part in parts], axis=0), axis=1, keepdims=True) / macro_total
            for plane in range(2)
        ],
        offset,
    )


VMEM = pl.BlockSpec(memory_space=pltpu.VMEM)
HBM = pl.BlockSpec(memory_space=pltpu.HBM)


def call(kernel, operands, outs, scratch=(), in_specs=None, out_specs=None, name=None):
    in_specs = in_specs or [VMEM] * len(operands)
    operands = [
        pltpu.with_memory_space_constraint(operand, pltpu.VMEM if spec is VMEM else pltpu.HBM)
        for operand, spec in zip(operands, in_specs)
    ]
    return pl.pallas_call(
        kernel,
        out_shape=outs,
        in_specs=in_specs,
        out_specs=out_specs or jax.tree.map(lambda out: VMEM, outs),
        scratch_shapes=list(scratch),
        compiler_params=pltpu.CompilerParams(vmem_limit_bytes=16 << 20),
        name=name,
    )(*operands)


def shape(dims, dtype=F32):
    return pltpu.VMEM(dims, dtype)


def swap_cores(value):
    return lax.ppermute(value, "mp", [(source, source ^ 1) for source in range(lax.axis_size("mp"))])


def over_bunches(value):
    size, inner = lax.axis_size("bunch"), lax.axis_size("mp")
    return [value] + [
        lax.ppermute(value, ("bunch", "mp"), [(source, (source ^ (step * inner)) ^ 1) for source in range(size * inner)])
        for step in range(1, size)
    ]


def over_macros(value):
    size = lax.axis_size("mp")
    chip = value + swap_cores(value)
    core = lax.axis_index("mp") % CORES
    steps = list(range(size // CORES - 1, 0, -1))
    received = []
    for first in reversed(range(0, len(steps), CORES)):
        taken = steps[first : first + CORES]
        hop = [taken[min(core_from, len(taken) - 1)] * CORES for core_from in range(CORES)]
        part = lax.ppermute(chip, "mp", [(source, (source ^ hop[source % CORES]) ^ 1) for source in range(size)])
        received.append(part if len(taken) == CORES else jnp.where(core == 0, part, 0.0))
    mine = total([jnp.where(core == 0, chip, 0.0)] + received)
    return mine, swap_cores(mine)


def body(phase_space, phase_advance, centroid_history, lr_wake, sr_dipole, sr_quad, slice_ids):
    _, own, macros = phase_space.shape
    depth = centroid_history.shape[1]
    all_bunches = own * lax.axis_size("bunch")
    wake = lr_wake.reshape(depth + 1, all_bunches)
    history = centroid_history.transpose(0, 2, 1).reshape(2 * own, depth)
    tiles = pl.cdiv(all_bunches, LANES)
    small_rows = tiles * SUBLANES
    split_shape = shape((4, macros // LANES, own, LANES))
    digit_shape = shape((macros // LANES, own, LANES), jnp.int32)
    moment_rows = 3 * HALVES * own

    message, split, low, high = call(
        start_kernel,
        (phase_space, slice_ids, history),
        (shape((small_rows + 2 * own, LANES)), split_shape, digit_shape, digit_shape),
        [
            pltpu.VMEM((2, own, macros), F32),
            pltpu.VMEM((own, macros), jnp.int32),
            pltpu.VMEM(history.shape, F32),
            pltpu.SemaphoreType.DMA((4,)),
        ],
        [HBM, HBM, HBM],
        name="start",
    )
    coords = phase_space
    later = earlier_centroid = None
    for turn in range(TURNS):
        last = turn == TURNS - 1
        gathered = over_bunches(message)
        moments = call(
            moments_kernel,
            (split, low, high),
            shape((3, HALVES, own, LANES)),
            [pltpu.VMEM((3 * HIGH * own, LOW), F32)],
            name="moments",
        )
        small = total([part[:small_rows] for part in gathered])
        mine, other = over_macros(jnp.concatenate([moments.reshape(moment_rows, LANES), small], axis=0))
        if turn == 0:
            low, high, turned, wakes, near, older = call(
                functools.partial(prepare_kernel, depth),
                [slice_ids, phase_advance, sr_dipole, sr_quad, wake] + gathered,
                (
                    digit_shape,
                    digit_shape,
                    shape((4, own, LANES)),
                    shape((2, 2, SLICES, SLICES), BF16),
                    shape((TURNS, tiles, own, LANES)),
                    shape((TURNS, 2, own, LANES)),
                ),
                name="prepare",
            )
        operands = (coords, slice_ids, mine, other, turned, wakes, near, older)
        table = pltpu.VMEM((3, HALVES, own, LANES), F32)
        if last:
            coords, centroids = call(
                functools.partial(apply_kernel, True),
                operands + (later, earlier_centroid),
                (jax.ShapeDtypeStruct(coords.shape, F32), jax.ShapeDtypeStruct((2, TURNS, own), F32)),
                [table, pltpu.VMEM(coords.shape, F32), pltpu.VMEM((2, TURNS, own), F32), pltpu.SemaphoreType.DMA((own // SUBLANES * pl.cdiv(macros, 1024) + 1,))],
                None,
                (HBM, HBM),
                name="apply_last",
            )
        else:
            coords, earlier_centroid, later, message, split = call(
                functools.partial(apply_kernel, False),
                operands,
                (shape(coords.shape), shape((2, own)), shape((2, own, LANES)), shape((small_rows, LANES)), split_shape),
                [table],
                name="apply",
            )
    return coords, centroids


def solution(mesh):
    placed = (
        P(None, "bunch", "mp"),
        P(None, "bunch"),
        P(None, None, "bunch"),
        P(),
        P(),
        P(),
        P(None, "bunch", "mp"),
    )
    return jax.shard_map(
        body,
        mesh=mesh,
        in_specs=placed,
        out_specs=(P(None, "bunch", "mp"), P(None, None, "bunch")),
        check_vma=False,
    )
```

```python
import functools

import jax
import jax.numpy as jnp
from jax import lax
from jax.experimental import pallas as pl
from jax.experimental.pallas import tpu as pltpu
from jax.sharding import PartitionSpec as P

SLICES = 256
TURNS = 2
DETUNE = 0.02
LOW = 32
HIGH = SLICES // LOW
LANES = 128
SUBLANES = 8
HALVES = SLICES // LANES
CORES = 2
HIGHEST = lax.Precision.HIGHEST
F32 = jnp.float32
BF16 = jnp.bfloat16


def iota(shape, axis):
    return lax.broadcasted_iota(jnp.int32, shape, axis)


def total(values):
    return functools.reduce(lambda a, b: a + b, values)


def rows_to_column(row, offset, count):
    length = row.shape[1]
    pick = iota((count, length), 1) == iota((count, length), 0) + offset
    return jnp.sum(jnp.where(pick, jnp.broadcast_to(row, (count, length)), 0.0), axis=1, keepdims=True)


def column_to_row(column, offset, length):
    count = column.shape[0]
    pick = iota((count, length), 1) == iota((count, length), 0) + offset
    return jnp.sum(jnp.where(pick, jnp.broadcast_to(column, (count, length)), 0.0), axis=0, keepdims=True)


def spread_far(weighted, offset):
    own, width = weighted.shape
    rows = iota((own, width), 0)
    step = 1
    while step < own:
        weighted = jnp.where((rows & step) != 0, pltpu.roll(weighted, step, 1), weighted)
        step *= 2
    return pltpu.roll(jnp.sum(weighted, axis=0, keepdims=True), width // 2 + 1 + offset, 1)


def gather_lanes(row, index):
    count = index.shape[0]
    result = jnp.zeros(index.shape, F32)
    for tile in range(row.shape[1] // LANES):
        part = jnp.broadcast_to(row[:, tile * LANES : (tile + 1) * LANES], (count, LANES))
        taken = jnp.take_along_axis(part, index & (LANES - 1), axis=1)
        result = jnp.where(index // LANES == tile, taken, result)
    return result


def store_centroids(small_ref, columns, offset):
    tiles = small_ref.shape[0] // SUBLANES
    rows = [column_to_row(column, offset, tiles * LANES) for column in columns]
    rows.append(jnp.zeros((SUBLANES - len(rows), tiles * LANES), F32))
    whole = jnp.concatenate(rows, axis=0)
    for tile in range(tiles):
        small_ref[tile * SUBLANES : (tile + 1) * SUBLANES, :] = whole[:, tile * LANES : (tile + 1) * LANES]


def wake_rows(wake):
    before = jnp.concatenate([jnp.zeros((1, wake.shape[1]), F32), wake[:-1]], axis=0)
    return jnp.concatenate([before, wake], axis=1)


def store_split(split_ref, plane, block, bunches, values):
    upper = values.astype(BF16).astype(F32)
    split_ref[2 * plane, block, bunches, :] = upper
    split_ref[2 * plane + 1, block, bunches, :] = values - upper


def store_digits(ids_of, low_ref, high_ref):
    for block in range(low_ref.shape[0]):
        ids = ids_of(slice(block * LANES, (block + 1) * LANES))
        low_ref[block] = ids & (LOW - 1)
        high_ref[block] = ids // LOW


def start_kernel(
    coords_hbm, slice_hbm, history_hbm, message_ref, split_ref, low_ref, high_ref, coords_ref, ids_ref, history_ref, sems
):
    own, macros = ids_ref.shape
    offset = lax.axis_index("bunch") * own
    macro_total = macros * lax.axis_size("mp")
    copies = [pltpu.make_async_copy(coords_hbm.at[2 * plane], coords_ref.at[plane], sems.at[plane]) for plane in range(2)]
    copies.append(pltpu.make_async_copy(slice_hbm.at[0], ids_ref, sems.at[2]))
    copies.append(pltpu.make_async_copy(history_hbm, history_ref, sems.at[3]))
    for copy in copies:
        copy.start()
    centroids = []
    for plane in range(2):
        copies[plane].wait()
        sums = jnp.zeros((own, LANES), F32)
        for block in range(macros // LANES):
            piece = coords_ref[plane, :, block * LANES : (block + 1) * LANES]
            store_split(split_ref, plane, block, slice(None), piece)
            sums += piece
        centroids.append(jnp.sum(sums, axis=1, keepdims=True) / macro_total)
    copies[2].wait()
    store_digits(lambda span: ids_ref[:, span], low_ref, high_ref)
    copies[3].wait()
    rows, depth = history_ref.shape
    first = message_ref.shape[0] - rows
    store_centroids(message_ref.at[:first, :], centroids, offset)
    message_ref[first:, :] = jnp.concatenate([history_ref[...], jnp.zeros((rows, LANES - depth), F32)], axis=1)


def moments_kernel(split_ref, low_ref, high_ref, out_ref, block_ref):
    _, blocks, own, _ = split_ref.shape
    step = min(8, blocks)
    chunk = step * LANES
    low_levels = iota((LOW, chunk), 0)
    high_levels = iota((HIGH, chunk), 0)

    def one_bunch(bunch, carry):
        sums = jnp.zeros((5 * HIGH, LOW), F32)
        for start in range(0, blocks, step):

            def line(ref):
                rows = pl.ds(bunch, HIGH, stride=0)
                return jnp.concatenate([ref[start + block, rows, :] for block in range(step)], axis=1)

            ids = line(low_ref)
            low = jnp.concatenate([ids] * (LOW // HIGH), axis=0) == low_levels
            high = line(high_ref) == high_levels
            parts = [jnp.where(high, line(split_ref.at[part]), 0.0) for part in range(4)]
            parts.append(jnp.where(high, 1.0, 0.0))
            sums += lax.dot_general(
                jnp.concatenate(parts, axis=0).astype(BF16),
                low.astype(F32).astype(BF16),
                (((1,), (1,)), ((), ())),
                preferred_element_type=F32,
            )
        kinds = (sums[4 * HIGH :], sums[:HIGH] + sums[HIGH : 2 * HIGH], sums[2 * HIGH : 3 * HIGH] + sums[3 * HIGH : 4 * HIGH])
        for kind in range(3):
            block_ref[pl.ds(kind * HIGH * own + bunch, HIGH, stride=own), :] = kinds[kind]
        return carry

    lax.fori_loop(0, own, one_bunch, 0, unroll=True)
    each = LANES // LOW
    for kind in range(3):
        for half in range(HALVES):
            first = (kind * HIGH + half * each) * own
            out_ref[kind, half] = jnp.concatenate(
                [block_ref[first + level * own : first + (level + 1) * own, :] for level in range(each)], axis=1
            )


def prepare_kernel(depth, slice_ref, advance_ref, dipole_wake_ref, quad_wake_ref, wake_ref, *refs):
    history_refs = refs[:-6]
    low_ref, high_ref, turned_ref, wakes_ref, near_ref, older_ref = refs[-6:]
    own = slice_ref.shape[1]
    all_bunches = wake_ref.shape[1]
    shard = lax.axis_index("bunch")
    offset = shard * own
    store_digits(lambda span: slice_ref[1, :, span], low_ref, high_ref)
    for index, ref in enumerate((dipole_wake_ref, quad_wake_ref)):
        whole = ref[...]
        upper = whole.astype(BF16)
        wakes_ref[index, 0] = upper
        wakes_ref[index, 1] = (whole - upper.astype(F32)).astype(BF16)
    for plane in range(2):
        line = advance_ref[plane : plane + 1, :]
        for index, values in enumerate((jnp.sin(line), jnp.cos(line))):
            turned_ref[2 * plane + index] = jnp.broadcast_to(rows_to_column(values, 0, own), (own, LANES))
    lags = wake_rows(wake_ref[...])
    for turn in range(TURNS):
        for tile in range(near_ref.shape[1]):
            other = iota((own, LANES), 1) + tile * LANES
            index = all_bunches - 1 + offset + iota((own, LANES), 0) - other
            taken = gather_lanes(lags[turn : turn + 1], jnp.where(other < all_bunches, index, 0))
            near_ref[turn, tile] = jnp.where(other < all_bunches, taken, 0.0)
    ahead = [lags[1:]]
    for turn in range(1, TURNS):
        ahead.append(jnp.concatenate([lags[1 + turn :], jnp.zeros((turn, 2 * all_bunches), F32)], axis=0))
    history = jnp.concatenate([ref[-2 * own :, :depth] for ref in history_refs], axis=0)
    older = jnp.dot(history, jnp.concatenate(ahead, axis=1), precision=HIGHEST, preferred_element_type=F32)
    first_lane = iota((own, LANES), 1) == 0
    for turn in range(TURNS):
        span = slice(turn * 2 * all_bunches, (turn + 1) * 2 * all_bunches)
        for plane in range(2):
            row = total(
                [
                    spread_far(older[(2 * step + plane) * own : (2 * step + plane + 1) * own, span], (shard ^ step) * own)
                    for step in range(len(history_refs))
                ]
            )
            older_ref[turn, plane] = jnp.where(first_lane, rows_to_column(row, offset, own), 0.0)


def sincos(angle):
    turns = jnp.floor(angle * 0.3183098861837907 + 0.5)
    rest = angle - turns * 3.140625
    rest = rest - turns * 9.67502593994140625e-4
    rest = rest - turns * 1.509957990978376432e-7
    rest = jnp.clip(rest, -1.75, 1.75)
    square = rest * rest
    sine = -2.3889859e-8
    for term in (2.7525562e-6, -1.9840874e-4, 8.3333310e-3, -1.6666667e-1):
        sine = sine * square + term
    sine = rest + rest * (square * sine)
    cosine = -2.6051615e-7
    for term in (2.4760495e-5, -1.3888378e-3, 4.1666638e-2, -0.5):
        cosine = cosine * square + term
    cosine = 1.0 + square * cosine
    half = turns * 0.5
    sign = jnp.where(half == jnp.floor(half), 1.0, -1.0)
    return sign * sine, sign * cosine


def wake_product(rows, wake_ref):
    contract = (((1,), (1,)), ((), ()))
    upper = rows.astype(BF16)
    lower = (rows - upper.astype(F32)).astype(BF16)
    both = jnp.concatenate([upper, lower], axis=0)
    count = rows.shape[0]
    first = lax.dot_general(both, wake_ref[0], contract, preferred_element_type=F32)
    second = lax.dot_general(upper, wake_ref[1], contract, preferred_element_type=F32)
    return first[:count] + first[count:] + second


def apply_kernel(last, coords_ref, slice_ref, mine_ref, other_ref, turned_ref, wakes_ref, near_ref, older_ref, *refs):
    turn = TURNS - 1 if last else 0
    _, own, macros = coords_ref.shape
    offset = lax.axis_index("bunch") * own
    macro_total = macros * lax.axis_size("mp")
    moment_rows = 3 * HALVES * own

    def both(first, count):
        return mine_ref[first : first + count, :] + other_ref[first : first + count, :]

    moments = [
        jnp.concatenate([both((kind * HALVES + half) * own, own) for half in range(HALVES)], axis=1) / macro_total
        for kind in range(3)
    ]
    small = [
        both(moment_rows + tile * SUBLANES, SUBLANES) for tile in range((mine_ref.shape[0] - moment_rows) // SUBLANES)
    ]
    if last:
        later_ref, earlier_centroid_ref, out_hbm_ref, centroid_hbm_ref, table_ref, out_ref, centroid_ref, out_sem = refs
    else:
        out_ref, centroid_ref, later_ref, small_out_ref, split_ref, table_ref = refs

    copies = []

    def far_of(lag, plane):
        return total(
            [near_ref[lag, tile] * jnp.broadcast_to(part[plane : plane + 1], (own, LANES)) for tile, part in enumerate(small)]
        )

    far = []
    for plane in range(2):
        past = later_ref[plane] if last else older_ref[0, plane]
        far.append(jnp.sum(far_of(0, plane) + past, axis=1, keepdims=True))
    dip_kick = wake_product(jnp.concatenate(moments[1:], axis=0), wakes_ref.at[0])
    quad_kick = wake_product(moments[0], wakes_ref.at[1])
    for kind, table in enumerate((dip_kick[:own] + far[0], dip_kick[own:] + far[1], quad_kick)):
        for half in range(HALVES):
            table_ref[kind, half] = table[:, half * LANES : (half + 1) * LANES]
    centroid = jnp.concatenate(
        [column_to_row(jnp.sum(moments[1 + plane], axis=1, keepdims=True), 0, own) for plane in range(2)], axis=0
    )
    if last:
        for plane in range(2):
            centroid_ref[plane] = jnp.concatenate(
                [earlier_centroid_ref[plane : plane + 1], centroid[plane : plane + 1]], axis=0
            )
        copies.append(pltpu.make_async_copy(centroid_ref, centroid_hbm_ref, out_sem.at[0]))
        copies[-1].start()
    else:
        centroid_ref[...] = centroid
        for plane in range(2):
            later_ref[plane] = far_of(1, plane) + older_ref[1, plane]

    chunk = min(1024, macros)
    parts = []
    for group in range(0, own, SUBLANES):
        bunches = pl.ds(group, SUBLANES)
        tables = [[table_ref[kind, half, bunches, :] for half in range(HALVES)] for kind in range(3)]
        turned = [turned_ref[index, bunches, :] for index in range(4)]

        def step(index, sums):
            for start in range(0, chunk, LANES):
                span = pl.ds(index * chunk + start, LANES)
                ids = slice_ref[turn, bunches, span]
                within = ids & (LANES - 1)
                upper = ids >= LANES
                picked = [
                    jnp.where(
                        upper,
                        jnp.take_along_axis(table[1], within, axis=1, mode="promise_in_bounds"),
                        jnp.take_along_axis(table[0], within, axis=1, mode="promise_in_bounds"),
                    )
                    for table in tables
                ]
                x, mx, y, my = (coords_ref[row, bunches, span] for row in range(4))
                mx = mx + picked[0] + picked[2] * x
                my = my + picked[1] - picked[2] * y
                action = x * x + mx * mx + y * y + my * my
                sine, cosine = sincos(DETUNE * action)
                new_sums = []
                for plane, (u, v) in enumerate(((x, mx), (y, my))):
                    sine_0, cosine_0 = turned[2 * plane : 2 * plane + 2]
                    full_sine = sine_0 * cosine + cosine_0 * sine
                    full_cosine = cosine_0 * cosine - sine_0 * sine
                    new_u = full_cosine * u + full_sine * v
                    out_ref[2 * plane, bunches, span] = new_u
                    out_ref[2 * plane + 1, bunches, span] = full_cosine * v - full_sine * u
                    if not last:
                        store_split(split_ref, plane, index * (chunk // LANES) + start // LANES, bunches, new_u)
                        new_sums.append(sums[plane] + new_u)
                sums = tuple(new_sums)
            return sums

        zero = jnp.zeros((SUBLANES, LANES), F32)
        sums = () if last else (zero, zero)
        for index in range(macros // chunk):
            sums = step(index, sums)
            if last:
                area = (slice(None), bunches, pl.ds(index * chunk, chunk))
                copies.append(pltpu.make_async_copy(out_ref.at[area], out_hbm_ref.at[area], out_sem.at[len(copies)]))
                copies[-1].start()
        parts.append(sums)
    if last:
        for copy in copies:
            copy.wait()
        return
    store_centroids(
        small_out_ref,
        [
            jnp.sum(jnp.concatenate([part[plane] for part in parts], axis=0), axis=1, keepdims=True) / macro_total
            for plane in range(2)
        ],
        offset,
    )


VMEM = pl.BlockSpec(memory_space=pltpu.VMEM)
HBM = pl.BlockSpec(memory_space=pltpu.HBM)


def call(kernel, operands, outs, scratch=(), in_specs=None, out_specs=None, name=None):
    in_specs = in_specs or [VMEM] * len(operands)
    operands = [
        pltpu.with_memory_space_constraint(operand, pltpu.VMEM if spec is VMEM else pltpu.HBM)
        for operand, spec in zip(operands, in_specs)
    ]
    return pl.pallas_call(
        kernel,
        out_shape=outs,
        in_specs=in_specs,
        out_specs=out_specs or jax.tree.map(lambda out: VMEM, outs),
        scratch_shapes=list(scratch),
        compiler_params=pltpu.CompilerParams(vmem_limit_bytes=16 << 20),
        name=name,
    )(*operands)


def shape(dims, dtype=F32):
    return pltpu.VMEM(dims, dtype)


def swap_cores(value):
    return lax.ppermute(value, "mp", [(source, source ^ 1) for source in range(lax.axis_size("mp"))])


def over_bunches(value):
    size, inner = lax.axis_size("bunch"), lax.axis_size("mp")
    return [value] + [
        lax.ppermute(value, ("bunch", "mp"), [(source, (source ^ (step * inner)) ^ 1) for source in range(size * inner)])
        for step in range(1, size)
    ]


def over_macros(value):
    size = lax.axis_size("mp")
    swapped = swap_cores(value)
    near = lax.ppermute(value, "mp", [(source, (source ^ CORES) ^ 1) for source in range(size)]) if size > CORES else 0.0
    chip = value + swapped
    mine = value + near
    for first in range(2, size // CORES, CORES):
        hop = [(first + core) * CORES for core in range(CORES)]
        mine = mine + lax.ppermute(chip, "mp", [(source, (source ^ hop[source % CORES]) ^ 1) for source in range(size)])
    return mine, swap_cores(mine)


def body(phase_space, phase_advance, centroid_history, lr_wake, sr_dipole, sr_quad, slice_ids):
    _, own, macros = phase_space.shape
    depth = centroid_history.shape[1]
    all_bunches = own * lax.axis_size("bunch")
    wake = lr_wake.reshape(depth + 1, all_bunches)
    history = centroid_history.transpose(0, 2, 1).reshape(2 * own, depth)
    tiles = pl.cdiv(all_bunches, LANES)
    small_rows = tiles * SUBLANES
    split_shape = shape((4, macros // LANES, own, LANES))
    digit_shape = shape((macros // LANES, own, LANES), jnp.int32)
    moment_rows = 3 * HALVES * own

    message, split, low, high = call(
        start_kernel,
        (phase_space, slice_ids, history),
        (shape((small_rows + 2 * own, LANES)), split_shape, digit_shape, digit_shape),
        [
            pltpu.VMEM((2, own, macros), F32),
            pltpu.VMEM((own, macros), jnp.int32),
            pltpu.VMEM(history.shape, F32),
            pltpu.SemaphoreType.DMA((4,)),
        ],
        [HBM, HBM, HBM],
        name="start",
    )
    coords = phase_space
    later = earlier_centroid = None
    for turn in range(TURNS):
        last = turn == TURNS - 1
        gathered = over_bunches(message)
        moments = call(
            moments_kernel,
            (split, low, high),
            shape((3, HALVES, own, LANES)),
            [pltpu.VMEM((3 * HIGH * own, LOW), F32)],
            name="moments",
        )
        small = total([part[:small_rows] for part in gathered])
        mine, other = over_macros(jnp.concatenate([moments.reshape(moment_rows, LANES), small], axis=0))
        if turn == 0:
            low, high, turned, wakes, near, older = call(
                functools.partial(prepare_kernel, depth),
                [slice_ids, phase_advance, sr_dipole, sr_quad, wake] + gathered,
                (
                    digit_shape,
                    digit_shape,
                    shape((4, own, LANES)),
                    shape((2, 2, SLICES, SLICES), BF16),
                    shape((TURNS, tiles, own, LANES)),
                    shape((TURNS, 2, own, LANES)),
                ),
                name="prepare",
            )
        operands = (coords, slice_ids, mine, other, turned, wakes, near, older)
        table = pltpu.VMEM((3, HALVES, own, LANES), F32)
        if last:
            coords, centroids = call(
                functools.partial(apply_kernel, True),
                operands + (later, earlier_centroid),
                (jax.ShapeDtypeStruct(coords.shape, F32), jax.ShapeDtypeStruct((2, TURNS, own), F32)),
                [table, pltpu.VMEM(coords.shape, F32), pltpu.VMEM((2, TURNS, own), F32), pltpu.SemaphoreType.DMA((own // SUBLANES * pl.cdiv(macros, 1024) + 1,))],
                None,
                (HBM, HBM),
                name="apply_last",
            )
        else:
            coords, earlier_centroid, later, message, split = call(
                functools.partial(apply_kernel, False),
                operands,
                (shape(coords.shape), shape((2, own)), shape((2, own, LANES)), shape((small_rows, LANES)), split_shape),
                [table],
                name="apply",
            )
    return coords, centroids


def solution(mesh):
    placed = (
        P(None, "bunch", "mp"),
        P(None, "bunch"),
        P(None, None, "bunch"),
        P(),
        P(),
        P(),
        P(None, "bunch", "mp"),
    )
    return jax.shard_map(
        body,
        mesh=mesh,
        in_specs=placed,
        out_specs=(P(None, "bunch", "mp"), P(None, None, "bunch")),
        check_vma=False,
    )
```

```python
import functools

import jax
import jax.numpy as jnp
from jax import lax
from jax.experimental import pallas as pl
from jax.experimental.pallas import tpu as pltpu
from jax.sharding import PartitionSpec as P

SLICES = 256
TURNS = 2
DETUNE = 0.02
LOW = 32
HIGH = SLICES // LOW
LANES = 128
SUBLANES = 8
HALVES = SLICES // LANES
CORES = 2
HIGHEST = lax.Precision.HIGHEST
F32 = jnp.float32
BF16 = jnp.bfloat16


def iota(shape, axis):
    return lax.broadcasted_iota(jnp.int32, shape, axis)


def total(values):
    return functools.reduce(lambda a, b: a + b, values)


def rows_to_column(row, offset, count):
    length = row.shape[1]
    pick = iota((count, length), 1) == iota((count, length), 0) + offset
    return jnp.sum(jnp.where(pick, jnp.broadcast_to(row, (count, length)), 0.0), axis=1, keepdims=True)


def column_to_row(column, offset, length):
    count = column.shape[0]
    pick = iota((count, length), 1) == iota((count, length), 0) + offset
    return jnp.sum(jnp.where(pick, jnp.broadcast_to(column, (count, length)), 0.0), axis=0, keepdims=True)


def spread_far(weighted, offset):
    own, width = weighted.shape
    rows = iota((own, width), 0)
    step = 1
    while step < own:
        weighted = jnp.where((rows & step) != 0, pltpu.roll(weighted, step, 1), weighted)
        step *= 2
    return pltpu.roll(jnp.sum(weighted, axis=0, keepdims=True), width // 2 + 1 + offset, 1)


def gather_lanes(row, index):
    count = index.shape[0]
    result = jnp.zeros(index.shape, F32)
    for tile in range(row.shape[1] // LANES):
        part = jnp.broadcast_to(row[:, tile * LANES : (tile + 1) * LANES], (count, LANES))
        taken = jnp.take_along_axis(part, index & (LANES - 1), axis=1)
        result = jnp.where(index // LANES == tile, taken, result)
    return result


def store_centroids(small_ref, columns, offset):
    tiles = small_ref.shape[0] // SUBLANES
    rows = [column_to_row(column, offset, tiles * LANES) for column in columns]
    rows.append(jnp.zeros((SUBLANES - len(rows), tiles * LANES), F32))
    whole = jnp.concatenate(rows, axis=0)
    for tile in range(tiles):
        small_ref[tile * SUBLANES : (tile + 1) * SUBLANES, :] = whole[:, tile * LANES : (tile + 1) * LANES]


def wake_rows(wake):
    before = jnp.concatenate([jnp.zeros((1, wake.shape[1]), F32), wake[:-1]], axis=0)
    return jnp.concatenate([before, wake], axis=1)


def store_split(split_ref, plane, block, bunches, values):
    upper = values.astype(BF16).astype(F32)
    split_ref[2 * plane, block, bunches, :] = upper
    split_ref[2 * plane + 1, block, bunches, :] = values - upper


def store_digits(ids_of, low_ref, high_ref):
    for block in range(low_ref.shape[0]):
        ids = ids_of(slice(block * LANES, (block + 1) * LANES))
        low_ref[block] = ids & (LOW - 1)
        high_ref[block] = ids // LOW


def packs(depth):
    return 2 * depth == LANES


def pack_planes(rows):
    count, depth = rows.shape
    if packs(depth):
        return jnp.concatenate([rows[: count // 2], rows[count // 2 :]], axis=1)
    return jnp.concatenate([rows, jnp.zeros((count, LANES - depth), F32)], axis=1)


def unpack_planes(packed, depth):
    if packs(depth):
        return jnp.concatenate([packed[:, :depth], packed[:, depth:]], axis=0)
    return packed[:, :depth]


def start_kernel(
    coords_hbm, slice_hbm, history_hbm, message_ref, split_ref, low_ref, high_ref, coords_ref, ids_ref, history_ref, sems
):
    own, macros = ids_ref.shape
    offset = lax.axis_index("bunch") * own
    macro_total = macros * lax.axis_size("mp")
    copies = [pltpu.make_async_copy(coords_hbm.at[2 * plane], coords_ref.at[plane], sems.at[plane]) for plane in range(2)]
    copies.append(pltpu.make_async_copy(slice_hbm.at[0], ids_ref, sems.at[2]))
    copies.append(pltpu.make_async_copy(history_hbm, history_ref, sems.at[3]))
    for copy in copies:
        copy.start()
    centroids = []
    for plane in range(2):
        copies[plane].wait()
        sums = jnp.zeros((own, LANES), F32)
        for block in range(macros // LANES):
            piece = coords_ref[plane, :, block * LANES : (block + 1) * LANES]
            store_split(split_ref, plane, block, slice(None), piece)
            sums += piece
        centroids.append(jnp.sum(sums, axis=1, keepdims=True) / macro_total)
    copies[2].wait()
    store_digits(lambda span: ids_ref[:, span], low_ref, high_ref)
    copies[3].wait()
    packed = pack_planes(history_ref[...])
    first = message_ref.shape[0] - packed.shape[0]
    store_centroids(message_ref.at[:first, :], centroids, offset)
    message_ref[first:, :] = packed


def moments_kernel(split_ref, low_ref, high_ref, out_ref, block_ref):
    _, blocks, own, _ = split_ref.shape
    step = min(8, blocks)
    chunk = step * LANES
    low_levels = iota((LOW, chunk), 0)
    high_levels = iota((HIGH, chunk), 0)

    def one_bunch(bunch, carry):
        sums = jnp.zeros((5 * HIGH, LOW), F32)
        for start in range(0, blocks, step):

            def line(ref):
                rows = pl.ds(bunch, HIGH, stride=0)
                return jnp.concatenate([ref[start + block, rows, :] for block in range(step)], axis=1)

            ids = line(low_ref)
            low = jnp.concatenate([ids] * (LOW // HIGH), axis=0) == low_levels
            high = line(high_ref) == high_levels
            parts = [jnp.where(high, line(split_ref.at[part]), 0.0) for part in range(4)]
            parts.append(jnp.where(high, 1.0, 0.0))
            sums += lax.dot_general(
                jnp.concatenate(parts, axis=0).astype(BF16),
                low.astype(F32).astype(BF16),
                (((1,), (1,)), ((), ())),
                preferred_element_type=F32,
            )
        kinds = (sums[4 * HIGH :], sums[:HIGH] + sums[HIGH : 2 * HIGH], sums[2 * HIGH : 3 * HIGH] + sums[3 * HIGH : 4 * HIGH])
        for kind in range(3):
            block_ref[pl.ds(kind * HIGH * own + bunch, HIGH, stride=own), :] = kinds[kind]
        return carry

    lax.fori_loop(0, own, one_bunch, 0, unroll=True)
    each = LANES // LOW
    for kind in range(3):
        for half in range(HALVES):
            first = (kind * HIGH + half * each) * own
            out_ref[kind, half] = jnp.concatenate(
                [block_ref[first + level * own : first + (level + 1) * own, :] for level in range(each)], axis=1
            )


def prepare_kernel(depth, slice_ref, advance_ref, dipole_wake_ref, quad_wake_ref, wake_ref, *refs):
    history_refs = refs[:-6]
    low_ref, high_ref, turned_ref, wakes_ref, near_ref, older_ref = refs[-6:]
    own = slice_ref.shape[1]
    all_bunches = wake_ref.shape[1]
    shard = lax.axis_index("bunch")
    offset = shard * own
    store_digits(lambda span: slice_ref[1, :, span], low_ref, high_ref)
    for index, ref in enumerate((dipole_wake_ref, quad_wake_ref)):
        whole = ref[...]
        upper = whole.astype(BF16)
        wakes_ref[index, 0] = upper
        wakes_ref[index, 1] = (whole - upper.astype(F32)).astype(BF16)
    for plane in range(2):
        line = advance_ref[plane : plane + 1, :]
        for index, values in enumerate((jnp.sin(line), jnp.cos(line))):
            turned_ref[2 * plane + index] = jnp.broadcast_to(rows_to_column(values, 0, own), (own, LANES))
    lags = wake_rows(wake_ref[...])
    for turn in range(TURNS):
        for tile in range(near_ref.shape[1]):
            other = iota((own, LANES), 1) + tile * LANES
            index = all_bunches - 1 + offset + iota((own, LANES), 0) - other
            taken = gather_lanes(lags[turn : turn + 1], jnp.where(other < all_bunches, index, 0))
            near_ref[turn, tile] = jnp.where(other < all_bunches, taken, 0.0)
    ahead = [lags[1:]]
    for turn in range(1, TURNS):
        ahead.append(jnp.concatenate([lags[1 + turn :], jnp.zeros((turn, 2 * all_bunches), F32)], axis=0))
    rows = own if packs(depth) else 2 * own
    history = jnp.concatenate([unpack_planes(ref[-rows:, :], depth) for ref in history_refs], axis=0)
    older = jnp.dot(history, jnp.concatenate(ahead, axis=1), precision=HIGHEST, preferred_element_type=F32)
    first_lane = iota((own, LANES), 1) == 0
    for turn in range(TURNS):
        span = slice(turn * 2 * all_bunches, (turn + 1) * 2 * all_bunches)
        for plane in range(2):
            row = total(
                [
                    spread_far(older[(2 * step + plane) * own : (2 * step + plane + 1) * own, span], (shard ^ step) * own)
                    for step in range(len(history_refs))
                ]
            )
            older_ref[turn, plane] = jnp.where(first_lane, rows_to_column(row, offset, own), 0.0)


def sincos(angle):
    turns = jnp.floor(angle * 0.3183098861837907 + 0.5)
    rest = angle - turns * 3.140625
    rest = rest - turns * 9.67502593994140625e-4
    rest = rest - turns * 1.509957990978376432e-7
    rest = jnp.clip(rest, -1.75, 1.75)
    square = rest * rest
    sine = -2.3889859e-8
    for term in (2.7525562e-6, -1.9840874e-4, 8.3333310e-3, -1.6666667e-1):
        sine = sine * square + term
    sine = rest + rest * (square * sine)
    cosine = -2.6051615e-7
    for term in (2.4760495e-5, -1.3888378e-3, 4.1666638e-2, -0.5):
        cosine = cosine * square + term
    cosine = 1.0 + square * cosine
    half = turns * 0.5
    sign = jnp.where(half == jnp.floor(half), 1.0, -1.0)
    return sign * sine, sign * cosine


def wake_product(rows, wake_ref):
    contract = (((1,), (1,)), ((), ()))
    upper = rows.astype(BF16)
    lower = (rows - upper.astype(F32)).astype(BF16)
    both = jnp.concatenate([upper, lower], axis=0)
    count = rows.shape[0]
    first = lax.dot_general(both, wake_ref[0], contract, preferred_element_type=F32)
    second = lax.dot_general(upper, wake_ref[1], contract, preferred_element_type=F32)
    return first[:count] + first[count:] + second


def apply_kernel(last, coords_ref, slice_ref, mine_ref, other_ref, turned_ref, wakes_ref, near_ref, older_ref, *refs):
    turn = TURNS - 1 if last else 0
    _, own, macros = coords_ref.shape
    offset = lax.axis_index("bunch") * own
    macro_total = macros * lax.axis_size("mp")
    moment_rows = 3 * HALVES * own

    def both(first, count):
        return mine_ref[first : first + count, :] + other_ref[first : first + count, :]

    moments = [
        jnp.concatenate([both((kind * HALVES + half) * own, own) for half in range(HALVES)], axis=1) / macro_total
        for kind in range(3)
    ]
    small = [
        both(moment_rows + tile * SUBLANES, SUBLANES) for tile in range((mine_ref.shape[0] - moment_rows) // SUBLANES)
    ]
    if last:
        later_ref, earlier_centroid_ref, out_hbm_ref, centroid_hbm_ref, table_ref, out_ref, centroid_ref, out_sem = refs
    else:
        out_ref, centroid_ref, later_ref, small_out_ref, split_ref, table_ref = refs

    copies = []

    def far_of(lag, plane):
        return total(
            [near_ref[lag, tile] * jnp.broadcast_to(part[plane : plane + 1], (own, LANES)) for tile, part in enumerate(small)]
        )

    far = []
    for plane in range(2):
        past = later_ref[plane] if last else older_ref[0, plane]
        far.append(jnp.sum(far_of(0, plane) + past, axis=1, keepdims=True))
    dip_kick = wake_product(jnp.concatenate(moments[1:], axis=0), wakes_ref.at[0])
    quad_kick = wake_product(moments[0], wakes_ref.at[1])
    for kind, table in enumerate((dip_kick[:own] + far[0], dip_kick[own:] + far[1], quad_kick)):
        for half in range(HALVES):
            table_ref[kind, half] = table[:, half * LANES : (half + 1) * LANES]
    centroid = jnp.concatenate(
        [column_to_row(jnp.sum(moments[1 + plane], axis=1, keepdims=True), 0, own) for plane in range(2)], axis=0
    )
    if last:
        for plane in range(2):
            centroid_ref[plane] = jnp.concatenate(
                [earlier_centroid_ref[plane : plane + 1], centroid[plane : plane + 1]], axis=0
            )
        copies.append(pltpu.make_async_copy(centroid_ref, centroid_hbm_ref, out_sem.at[0]))
        copies[-1].start()
    else:
        centroid_ref[...] = centroid
        for plane in range(2):
            later_ref[plane] = far_of(1, plane) + older_ref[1, plane]

    chunk = min(1024, macros)
    parts = []
    for group in range(0, own, SUBLANES):
        bunches = pl.ds(group, SUBLANES)
        tables = [[table_ref[kind, half, bunches, :] for half in range(HALVES)] for kind in range(3)]
        turned = [turned_ref[index, bunches, :] for index in range(4)]

        def step(index, sums):
            for start in range(0, chunk, LANES):
                span = pl.ds(index * chunk + start, LANES)
                ids = slice_ref[turn, bunches, span]
                within = ids & (LANES - 1)
                upper = ids >= LANES
                picked = [
                    jnp.where(
                        upper,
                        jnp.take_along_axis(table[1], within, axis=1, mode="promise_in_bounds"),
                        jnp.take_along_axis(table[0], within, axis=1, mode="promise_in_bounds"),
                    )
                    for table in tables
                ]
                x, mx, y, my = (coords_ref[row, bunches, span] for row in range(4))
                mx = mx + picked[0] + picked[2] * x
                my = my + picked[1] - picked[2] * y
                action = x * x + mx * mx + y * y + my * my
                sine, cosine = sincos(DETUNE * action)
                new_sums = []
                for plane, (u, v) in enumerate(((x, mx), (y, my))):
                    sine_0, cosine_0 = turned[2 * plane : 2 * plane + 2]
                    full_sine = sine_0 * cosine + cosine_0 * sine
                    full_cosine = cosine_0 * cosine - sine_0 * sine
                    new_u = full_cosine * u + full_sine * v
                    out_ref[2 * plane, bunches, span] = new_u
                    out_ref[2 * plane + 1, bunches, span] = full_cosine * v - full_sine * u
                    if not last:
                        store_split(split_ref, plane, index * (chunk // LANES) + start // LANES, bunches, new_u)
                        new_sums.append(sums[plane] + new_u)
                sums = tuple(new_sums)
            return sums

        zero = jnp.zeros((SUBLANES, LANES), F32)
        sums = () if last else (zero, zero)
        for index in range(macros // chunk):
            sums = step(index, sums)
            if last:
                area = (slice(None), bunches, pl.ds(index * chunk, chunk))
                copies.append(pltpu.make_async_copy(out_ref.at[area], out_hbm_ref.at[area], out_sem.at[len(copies)]))
                copies[-1].start()
        parts.append(sums)
    if last:
        for copy in copies:
            copy.wait()
        return
    store_centroids(
        small_out_ref,
        [
            jnp.sum(jnp.concatenate([part[plane] for part in parts], axis=0), axis=1, keepdims=True) / macro_total
            for plane in range(2)
        ],
        offset,
    )


VMEM = pl.BlockSpec(memory_space=pltpu.VMEM)
HBM = pl.BlockSpec(memory_space=pltpu.HBM)


def call(kernel, operands, outs, scratch=(), in_specs=None, out_specs=None, name=None):
    in_specs = in_specs or [VMEM] * len(operands)
    operands = [
        pltpu.with_memory_space_constraint(operand, pltpu.VMEM if spec is VMEM else pltpu.HBM)
        for operand, spec in zip(operands, in_specs)
    ]
    return pl.pallas_call(
        kernel,
        out_shape=outs,
        in_specs=in_specs,
        out_specs=out_specs or jax.tree.map(lambda out: VMEM, outs),
        scratch_shapes=list(scratch),
        compiler_params=pltpu.CompilerParams(vmem_limit_bytes=16 << 20),
        name=name,
    )(*operands)


def shape(dims, dtype=F32):
    return pltpu.VMEM(dims, dtype)


def swap_cores(value):
    return lax.ppermute(value, "mp", [(source, source ^ 1) for source in range(lax.axis_size("mp"))])


def over_bunches(value):
    size, inner = lax.axis_size("bunch"), lax.axis_size("mp")
    return [value] + [
        lax.ppermute(value, ("bunch", "mp"), [(source, (source ^ (step * inner)) ^ 1) for source in range(size * inner)])
        for step in range(1, size)
    ]


def over_macros(value):
    size = lax.axis_size("mp")
    swapped = swap_cores(value)
    near = lax.ppermute(value, "mp", [(source, (source ^ CORES) ^ 1) for source in range(size)]) if size > CORES else 0.0
    chip = value + swapped
    mine = value + near
    for first in range(2, size // CORES, CORES):
        hop = [(first + core) * CORES for core in range(CORES)]
        mine = mine + lax.ppermute(chip, "mp", [(source, (source ^ hop[source % CORES]) ^ 1) for source in range(size)])
    return mine, swap_cores(mine)


def body(phase_space, phase_advance, centroid_history, lr_wake, sr_dipole, sr_quad, slice_ids):
    _, own, macros = phase_space.shape
    depth = centroid_history.shape[1]
    all_bunches = own * lax.axis_size("bunch")
    wake = lr_wake.reshape(depth + 1, all_bunches)
    history = centroid_history.transpose(0, 2, 1).reshape(2 * own, depth)
    tiles = pl.cdiv(all_bunches, LANES)
    small_rows = tiles * SUBLANES
    split_shape = shape((4, macros // LANES, own, LANES))
    digit_shape = shape((macros // LANES, own, LANES), jnp.int32)
    moment_rows = 3 * HALVES * own

    message, split, low, high = call(
        start_kernel,
        (phase_space, slice_ids, history),
        (shape((small_rows + (own if packs(depth) else 2 * own), LANES)), split_shape, digit_shape, digit_shape),
        [
            pltpu.VMEM((2, own, macros), F32),
            pltpu.VMEM((own, macros), jnp.int32),
            pltpu.VMEM(history.shape, F32),
            pltpu.SemaphoreType.DMA((4,)),
        ],
        [HBM, HBM, HBM],
        name="start",
    )
    coords = phase_space
    later = earlier_centroid = None
    for turn in range(TURNS):
        last = turn == TURNS - 1
        gathered = over_bunches(message)
        moments = call(
            moments_kernel,
            (split, low, high),
            shape((3, HALVES, own, LANES)),
            [pltpu.VMEM((3 * HIGH * own, LOW), F32)],
            name="moments",
        )
        small = total([part[:small_rows] for part in gathered])
        mine, other = over_macros(jnp.concatenate([moments.reshape(moment_rows, LANES), small], axis=0))
        if turn == 0:
            low, high, turned, wakes, near, older = call(
                functools.partial(prepare_kernel, depth),
                [slice_ids, phase_advance, sr_dipole, sr_quad, wake] + gathered,
                (
                    digit_shape,
                    digit_shape,
                    shape((4, own, LANES)),
                    shape((2, 2, SLICES, SLICES), BF16),
                    shape((TURNS, tiles, own, LANES)),
                    shape((TURNS, 2, own, LANES)),
                ),
                name="prepare",
            )
        operands = (coords, slice_ids, mine, other, turned, wakes, near, older)
        table = pltpu.VMEM((3, HALVES, own, LANES), F32)
        if last:
            coords, centroids = call(
                functools.partial(apply_kernel, True),
                operands + (later, earlier_centroid),
                (jax.ShapeDtypeStruct(coords.shape, F32), jax.ShapeDtypeStruct((2, TURNS, own), F32)),
                [table, pltpu.VMEM(coords.shape, F32), pltpu.VMEM((2, TURNS, own), F32), pltpu.SemaphoreType.DMA((own // SUBLANES * pl.cdiv(macros, 1024) + 1,))],
                None,
                (HBM, HBM),
                name="apply_last",
            )
        else:
            coords, earlier_centroid, later, message, split = call(
                functools.partial(apply_kernel, False),
                operands,
                (shape(coords.shape), shape((2, own)), shape((2, own, LANES)), shape((small_rows, LANES)), split_shape),
                [table],
                name="apply",
            )
    return coords, centroids


def solution(mesh):
    placed = (
        P(None, "bunch", "mp"),
        P(None, "bunch"),
        P(None, None, "bunch"),
        P(),
        P(),
        P(),
        P(None, "bunch", "mp"),
    )
    return jax.shard_map(
        body,
        mesh=mesh,
        in_specs=placed,
        out_specs=(P(None, "bunch", "mp"), P(None, None, "bunch")),
        check_vma=False,
    )
```
